256 devices in a mesh: prow: 32 (over z_hi, y, x), pcol: 8 (over z_lo, core).
Axes of the slice: x: 4, y: 4, z: 8 (z_hi: 2, z_lo: 4; z = z_hi * 4 + z_lo), core: 2. Of those that a mesh axis runs over, the one named last changes fastest.
Arguments:
- eigen_rows: float32 [1024, 229376], P(('pcol', 'prow')), may hold values from -6 to 6
- reflectors: float32 [229376, 512], P('prow', 'pcol'), may hold values from -0.375 to 0.375
- tfactors: float32 [2, 256, 256], replicated, may hold values from -0.01171875 to 0.01171875
Outputs:
- back_rows: float32 [1024, 229376], P('pcol', 'prow')
The draws below stay inside these ranges and needn't reach their ends.
All inputs are finite; a program needn't handle non-finite values.
Results may differ from the reference program's by a relative error of at most 0.000084.
Values sent between devices are 32-bit elements; how exact they have to be, the bound alone decides.
No kernel may reach another device: no remote copies, remote signals or barrier semaphores. Data moves between devices by JAX's collectives and lax.ppermute only.
A program may use at most 128 MiB of HBM per device.

```python
import jax
import jax.numpy as jnp
from jax import lax

N = 229376
K = 1024
NB = 256


def level_of(stream_key, shape, pieces, smallest, largest):
    loudness = 1.0
    for dim, blocks in pieces:
        steps = jax.random.uniform(jax.random.fold_in(jax.random.fold_in(stream_key, 6), dim), (blocks,), jnp.float32, smallest / len(pieces), largest / len(pieces))
        loudness = loudness * jnp.repeat(jnp.exp(steps), shape[dim] // blocks).reshape((-1,) + (1,) * (len(shape) - 1 - dim))
    return loudness


def centred(rng, extent, scale, most, shards=(), dtype=jnp.bfloat16):
    result = jax.random.normal(rng, extent, jnp.float32) * scale
    if len(shards) > 0:
        result = level_of(rng, extent, shards, -0.22, 0.18) * result
    return jnp.clip(result, min=-most, max=most).astype(dtype)


def setup_inputs(seed: int = 0) -> dict:
    seeds = jax.random.split(jax.random.key(seed), 4)
    return {
        "eigen_rows": centred(seeds[0], (K, N), 1.0, 6.0, ((0, 256),), jnp.float32),
        "reflectors": centred(seeds[1], (N, 2 * NB), NB ** -0.5, 0.375, ((0, 32), (1, 8)), jnp.float32),
        "tfactors": centred(seeds[2], (2, NB, NB), N ** -0.5, 0.01171875, (), jnp.float32),
    }


def upper_part(square):
    width = square.shape[0]
    rows = lax.broadcasted_iota(jnp.int32, (width, width), 0)
    cols = lax.broadcasted_iota(jnp.int32, (width, width), 1)
    return jnp.where(cols >= rows, square, jnp.zeros_like(square))


def apply_panel(matrix, vectors, triangle):
    hp = lax.Precision.HIGHEST
    projected = jnp.dot(matrix, vectors, precision=hp, preferred_element_type=jnp.float32)
    scaled = jnp.dot(projected, triangle.T, precision=hp, preferred_element_type=jnp.float32)
    return matrix - jnp.dot(scaled, vectors.T, precision=hp, preferred_element_type=jnp.float32)


def reference(eigen_rows, reflectors, tfactors):
    first = reflectors[:, :NB]
    second = reflectors[:, NB:]
    middle = apply_panel(eigen_rows, second, upper_part(tfactors[1]))
    return apply_panel(middle, first, upper_part(tfactors[0]))
```

```python
import jax
import jax.numpy as jnp
from jax import lax
from jax.sharding import PartitionSpec as P


def upper_part(square):
    width = square.shape[0]
    rows = lax.broadcasted_iota(jnp.int32, (width, width), 0)
    cols = lax.broadcasted_iota(jnp.int32, (width, width), 1)
    return jnp.where(cols >= rows, square, jnp.zeros_like(square))


def matmul(left, right, precision=lax.Precision.HIGHEST):
    return jnp.dot(left, right, precision=precision, preferred_element_type=jnp.float32)


def sum_over_prow(values, members):
    slices = values.reshape((members, -1, 128))
    received = lax.all_to_all(slices, "prow", split_axis=0, concat_axis=0, tiled=True)
    total = jnp.sum(received, axis=0, keepdims=True)
    copies = jnp.broadcast_to(total, slices.shape)
    return lax.all_to_all(copies, "prow", split_axis=0, concat_axis=0, tiled=True)


def body(eigen_rows, reflectors, tfactors):
    members = lax.axis_size("prow")
    width = tfactors.shape[1]
    vectors = lax.all_gather(reflectors, "pcol", axis=1, tiled=True)
    rows = lax.all_to_all(eigen_rows, "prow", split_axis=1, concat_axis=0, tiled=True)
    count = rows.shape[0]
    first_tri = upper_part(tfactors[0])
    second_tri = upper_part(tfactors[1])
    fast = lax.Precision.HIGH

    projected = matmul(rows, vectors, fast)
    cross = matmul(vectors[:, width:].T, vectors[:, :width], fast)
    packed = jnp.concatenate(
        [projected.reshape(members, -1), cross.reshape(members, -1)], axis=1
    )
    packed = sum_over_prow(packed, members).reshape(packed.shape)
    split = projected.size // members
    projected = packed[:, :split].reshape(count, 2 * width)
    cross = packed[:, split:].reshape(width, width)
    scaled_second = matmul(projected[:, width:], second_tri.T)
    first = projected[:, :width] - matmul(scaled_second, cross)
    scaled_first = matmul(first, first_tri.T)
    scaled = jnp.concatenate([scaled_first, scaled_second], axis=1)
    return rows - matmul(scaled, vectors.T, fast)


def solution(mesh):
    return jax.shard_map(
        body,
        mesh=mesh,
        in_specs=(P(("pcol", "prow"), None), P("prow", "pcol"), P()),
        out_specs=P("pcol", "prow"),
        check_vma=False,
    )
```

```python
import jax
import jax.numpy as jnp
from jax import lax
from jax.sharding import PartitionSpec as P

UP_ONE = [(c, c + 2) for c in range(6)]
DOWN_ONE = [(c, c - 2) for c in range(2, 8)]
UP_TWO = [(c, c + 2) for c in range(2, 6)]
DOWN_TWO = [(c, c - 2) for c in range(2, 6)]
UP_END = [(4, 6), (5, 7)]
DOWN_END = [(2, 0), (3, 1)]
SIBLING = [(c, c ^ 1) for c in range(8)]
FAR = [(r, (r + 16) % 32) for r in range(32)]
PLANES = [list(range(16)), list(range(16, 32))]


def along_x(step):
    return [(r, r // 4 * 4 + (r + step) % 4) for r in range(32)]


def along_y(step):
    return [(r, r // 16 * 16 + (r + 4 * step) % 16) for r in range(32)]


def upper_part(square):
    width = square.shape[0]
    rows = lax.broadcasted_iota(jnp.int32, (width, width), 0)
    cols = lax.broadcasted_iota(jnp.int32, (width, width), 1)
    return jnp.where(cols >= rows, square, jnp.zeros_like(square))


def matmul(left, right, precision=lax.Precision.HIGHEST):
    return jnp.dot(left, right, precision=precision, preferred_element_type=jnp.float32)


def matmul_nt(left, right):
    return lax.dot_general(
        left, right, (((1,), (1,)), ((), ())),
        precision=lax.Precision.HIGH, preferred_element_type=jnp.float32,
    )


def sum_over_prow(values):
    x = lax.axis_index("prow") % 4
    quarters = values.reshape(4, -1, 128)

    def send(value, pairs):
        return lax.ppermute(value, "prow", pairs)

    def quarter(step):
        return lax.dynamic_index_in_dim(quarters, (x + step) % 4, 0, keepdims=False)

    total = quarter(0)
    for step in (1, 2, 3):
        total = total + send(quarter(step), along_x(step))
    total = total + send(total, along_y(1)) + send(total, along_y(2)) + send(total, along_y(3))
    total = total + send(total, FAR)
    others = [send(total, along_x(4 - step)) for step in (1, 2, 3)]
    ring = jnp.stack([total, *others] * 2)
    return lax.dynamic_slice_in_dim(ring, (4 - x) % 4, 4, 0).reshape(values.shape)


def body(eigen_rows, reflectors, tfactors):
    width = tfactors.shape[1]
    count = eigen_rows.shape[0]
    half = lax.axis_index("prow") // 16
    column = lax.axis_index("pcol")
    chip, core = column // 2, column % 2
    length = reflectors.shape[0]
    mine = reflectors.T

    def send(value, pairs):
        return lax.ppermute(value, "pcol", pairs)

    blocks = eigen_rows.reshape(count, 32, length).transpose(1, 0, 2)
    leaving = lax.dynamic_slice_in_dim(blocks, (1 - half) * 16, 16, 0)
    staying = lax.dynamic_slice_in_dim(blocks, half * 16, 16, 0)
    mine, leaving = lax.optimization_barrier((mine, leaving))
    arriving = lax.ppermute(leaving, "prow", FAR)
    below = send(mine, UP_ONE)
    above = send(mine, DOWN_ONE)

    def over_plane(value):
        value = lax.all_to_all(
            value, "prow", split_axis=0, concat_axis=0, tiled=True, axis_index_groups=PLANES
        )
        return value.reshape(16 * count, length)

    staying = over_plane(staying)
    below_two = send(below, UP_TWO)
    above_two = send(above, DOWN_TWO)
    arriving = over_plane(arriving)
    rows = jnp.concatenate(
        [jnp.where(half == 0, staying, arriving), jnp.where(half == 0, arriving, staying)], axis=0
    )
    last = send(below_two, UP_END) + send(above_two, DOWN_END)
    two = below_two + above_two

    def both_cores(piece):
        other = send(piece, SIBLING)
        return jnp.concatenate(
            [jnp.where(core == 0, piece, other), jnp.where(core == 0, other, piece)], axis=0
        )

    all_mine, all_below, all_above, all_two, all_last = (
        both_cores(piece) for piece in (mine, below, above, two, last)
    )

    left = jnp.where(chip == 0, two, jnp.where(chip == 3, mine, above))
    right = jnp.where(chip == 0, all_above, jnp.where(chip == 1, all_below, all_two))
    cross = sum_over_prow(matmul_nt(left, right))
    cross = lax.all_to_all(
        jnp.broadcast_to(cross, (8, *cross.shape)), "pcol", split_axis=0, concat_axis=0, tiled=True
    ).reshape(4, 128, 128)
    cross = jnp.concatenate(
        [
            jnp.concatenate([cross[1], cross[0]], axis=1),
            jnp.concatenate([cross[2], cross[3]], axis=1),
        ],
        axis=0,
    )

    zero = jnp.zeros_like
    on_last = matmul_nt(rows, all_last)
    on_above = matmul_nt(rows, all_above) + jnp.where(chip == 3, on_last, zero(on_last))
    on_below = matmul_nt(rows, all_below) + jnp.where(chip == 0, on_last, zero(on_last))
    slots = [matmul_nt(rows, all_mine), on_above, matmul_nt(rows, all_two), on_below]
    slots = sum_over_prow(jnp.concatenate(slots, axis=0)).reshape(4, -1, 128)

    def turned(parts, start):
        return lax.dynamic_slice_in_dim(jnp.concatenate([parts, parts], axis=0), start, 4, 0)

    ordered = turned(slots, (4 - chip) % 4)
    first = jnp.concatenate([ordered[0], ordered[1]], axis=1)
    second = jnp.concatenate([ordered[2], ordered[3]], axis=1)
    scaled_second = matmul(second, upper_part(tfactors[1]).T)
    scaled_first = matmul(first - matmul(scaled_second, cross), upper_part(tfactors[0]).T)
    scaled = jnp.stack(
        [scaled_first[:, :128], scaled_first[:, 128:], scaled_second[:, :128], scaled_second[:, 128:]]
    )
    scaled = turned(scaled, chip).transpose(1, 0, 2).reshape(-1, 2 * width)
    at_above = all_above + jnp.where(chip == 3, all_last, zero(all_last))
    at_below = all_below + jnp.where(chip == 0, all_last, zero(all_last))
    vectors = jnp.concatenate([all_mine, at_above, all_two, at_below], axis=0)
    return rows - matmul(scaled, vectors, lax.Precision.HIGH)


def solution(mesh):
    return jax.shard_map(
        body,
        mesh=mesh,
        in_specs=(P(("pcol", "prow"), None), P("prow", "pcol"), P()),
        out_specs=P("pcol", "prow"),
        check_vma=False,
    )
```

```python
import functools

import jax
import jax.numpy as jnp
from jax import lax
from jax.experimental import pallas as pl
from jax.experimental.pallas import tpu as pltpu
from jax.sharding import PartitionSpec as P

UP_ONE = [(c, c + 2) for c in range(6)]
DOWN_ONE = [(c, c - 2) for c in range(2, 8)]
UP_TWO = [(c, c + 2) for c in range(2, 6)]
DOWN_TWO = [(c, c - 2) for c in range(2, 6)]
UP_END = [(4, 6), (5, 7)]
DOWN_END = [(2, 0), (3, 1)]
SIBLING = [(c, c ^ 1) for c in range(8)]
FAR = [(r, (r + 16) % 32) for r in range(32)]
PLANES = [list(range(16)), list(range(16, 32))]


def along_x(step):
    return [(r, r // 4 * 4 + (r + step) % 4) for r in range(32)]


def along_y(step):
    return [(r, r // 16 * 16 + (r + 4 * step) % 16) for r in range(32)]


def upper_part(square):
    width = square.shape[0]
    rows = lax.broadcasted_iota(jnp.int32, (width, width), 0)
    cols = lax.broadcasted_iota(jnp.int32, (width, width), 1)
    return jnp.where(cols >= rows, square, jnp.zeros_like(square))


def matmul(left, right, precision=lax.Precision.HIGHEST):
    return jnp.dot(left, right, precision=precision, preferred_element_type=jnp.float32)


def matmul_nt(left, right):
    return lax.dot_general(
        left, right, (((1,), (1,)), ((), ())),
        precision=lax.Precision.HIGH, preferred_element_type=jnp.float32,
    )


def sum_over_prow(values):
    x = lax.axis_index("prow") % 4

    def send(value, pairs):
        return lax.ppermute(value, "prow", pairs)

    def quarter(step):
        return lax.dynamic_index_in_dim(values, (x + step) % 4, 0, keepdims=False)

    total = quarter(0)
    for step in (1, 2, 3):
        total = total + send(quarter(step), along_x(step))
    total = total + send(total, along_y(1)) + send(total, along_y(2)) + send(total, along_y(3))
    far = send(total, FAR)
    total = total + jnp.concatenate([far[64:128], far[:64], far[128:]], axis=0)
    return jnp.stack([total, *(send(total, along_x(4 - step)) for step in (1, 2, 3))])


def turned(parts, start):
    return lax.dynamic_slice_in_dim(jnp.concatenate([parts, parts], axis=0), start % 4, 4, 0)


def split(value):
    high = lax.reduce_precision(value, 8, 7)
    return high.astype(jnp.bfloat16), (value - high).astype(jnp.bfloat16)


def update_kernel(half_ref, rows_ref, scaled_ref, *refs):
    out_ref = refs[-1]
    high = [ref[...] for ref in refs[:4]]
    low = [ref[...] for ref in refs[4:8]]
    count = rows_ref.shape[0]
    dot = functools.partial(jnp.dot, preferred_element_type=jnp.float32)
    change = None
    for pair in (0, 1):
        columns = slice(256 * pair, 256 * pair + 256)
        left = scaled_ref[:, columns]
        both = dot(left, jnp.concatenate(high[2 * pair : 2 * pair + 2], axis=0))
        part = both[:count] + both[count:]
        part = part + dot(left[:count], jnp.concatenate(low[2 * pair : 2 * pair + 2], axis=0))
        change = part if change is None else change + part
    result = rows_ref[...] - change
    mid = count // 2
    here = pl.multiple_of(half_ref[0] * mid, mid)
    there = pl.multiple_of((1 - half_ref[0]) * mid, mid)
    out_ref[pl.ds(here, mid), :] = result[:mid]
    out_ref[pl.ds(there, mid), :] = result[mid:]


def update(half, rows, scaled, high, low):
    count, length = rows.shape
    tile = 1024
    block = pl.BlockSpec((128, tile), lambda i, h: (0, i))
    return pl.pallas_call(
        update_kernel,
        out_shape=jax.ShapeDtypeStruct(rows.shape, jnp.float32),
        grid_spec=pltpu.PrefetchScalarGridSpec(
            num_scalar_prefetch=1,
            grid=(length // tile,),
            in_specs=[
                pl.BlockSpec((count, tile), lambda i, h: (0, i)),
                pl.BlockSpec(scaled.shape, lambda i, h: (0, 0)),
                *[block] * 8,
            ],
            out_specs=pl.BlockSpec((count, tile), lambda i, h: (0, i)),
        ),
        compiler_params=pltpu.CompilerParams(vmem_limit_bytes=32 * 1024 * 1024),
        cost_estimate=pl.CostEstimate(
            flops=6 * count * 512 * length, bytes_accessed=length * (512 * 4 + count * 8), transcendentals=0
        ),
    )(half.reshape(1), rows, scaled, *high, *low)


def body(eigen_rows, reflectors, tfactors):
    count = eigen_rows.shape[0]
    prow = lax.axis_index("prow")
    x, half = prow % 4, prow // 16
    column = lax.axis_index("pcol")
    chip, core = column // 2, column % 2
    length = reflectors.shape[0]
    mine = reflectors.T

    def send(value, pairs):
        return lax.ppermute(value, "pcol", pairs)

    def ordered(piece, other, axis):
        return jnp.concatenate(
            [jnp.where(core == 0, piece, other), jnp.where(core == 0, other, piece)], axis=axis
        )

    def both_cores(piece):
        return ordered(piece, send(piece, SIBLING), 0)

    blocks = eigen_rows.reshape(count, 32, length).transpose(1, 0, 2)
    leaving = lax.dynamic_slice_in_dim(blocks, (1 - half) * 16, 16, 0)
    staying = lax.dynamic_slice_in_dim(blocks, half * 16, 16, 0)
    mine, leaving = lax.optimization_barrier((mine, leaving))
    arriving = lax.ppermute(leaving, "prow", FAR)
    below = send(mine, UP_ONE)
    above = send(mine, DOWN_ONE)

    def over_plane(value):
        value = lax.all_to_all(
            value, "prow", split_axis=0, concat_axis=0, tiled=True, axis_index_groups=PLANES
        )
        return value.reshape(16 * count, length)

    staying = over_plane(staying)
    below_two = send(below, UP_TWO)
    above_two = send(above, DOWN_TWO)
    arriving, below_two, above_two = lax.optimization_barrier((arriving, below_two, above_two))
    below_end = send(below_two, UP_END)
    above_end = send(above_two, DOWN_END)
    arriving = over_plane(arriving)
    rows = jnp.concatenate([staying, arriving], axis=0)
    two = below_two + above_two

    all_mine, all_below, all_above, all_two = (
        both_cores(piece) for piece in (mine, below, above, two)
    )

    left = jnp.where(chip == 0, two, jnp.where(chip == 3, mine, above))
    right = jnp.where(chip == 0, all_above, jnp.where(chip == 1, all_below, all_two))
    cross = matmul_nt(left, right)
    on_mine, on_two = matmul_nt(rows, all_mine), matmul_nt(rows, all_two)
    on_above, on_below = matmul_nt(rows, all_above), matmul_nt(rows, all_below)
    below_end, above_end, cross, on_mine, on_two, on_above, on_below = lax.optimization_barrier(
        (below_end, above_end, cross, on_mine, on_two, on_above, on_below)
    )

    last = below_end + above_end
    last_other = send(last, SIBLING)
    zero = jnp.zeros_like
    on_last = ordered(matmul_nt(rows, last), matmul_nt(rows, last_other), 1)
    slots = jnp.stack(
        [
            on_mine,
            on_above + jnp.where(chip == 3, on_last, zero(on_last)),
            on_two,
            on_below + jnp.where(chip == 0, on_last, zero(on_last)),
        ]
    )
    summed = sum_over_prow(jnp.concatenate([slots, cross.reshape(4, 16, 128)], axis=1))
    cross = turned(summed[:, 128:], 4 - x).reshape(64, 128)
    cross = lax.all_to_all(
        jnp.broadcast_to(cross, (8, *cross.shape)), "pcol", split_axis=0, concat_axis=0, tiled=True
    ).reshape(4, 128, 128)
    cross = jnp.concatenate(
        [
            jnp.concatenate([cross[1], cross[0]], axis=1),
            jnp.concatenate([cross[2], cross[3]], axis=1),
        ],
        axis=0,
    )
    projected = turned(summed[:, :128], 8 - chip - x)
    first = jnp.concatenate([projected[0], projected[1]], axis=1)
    second = jnp.concatenate([projected[2], projected[3]], axis=1)
    scaled_second = matmul(second, upper_part(tfactors[1]).T)
    scaled_first = matmul(first - matmul(scaled_second, cross), upper_part(tfactors[0]).T)
    scaled = jnp.stack(
        [scaled_first[:, :128], scaled_first[:, 128:], scaled_second[:, :128], scaled_second[:, 128:]]
    )
    scaled = turned(scaled, chip)
    scaled = jnp.concatenate([scaled[j] for j in range(4)], axis=1)
    scaled = jnp.concatenate(split(scaled), axis=0)

    all_last = ordered(last, last_other, 0)
    at_above = all_above + jnp.where(chip == 3, all_last, zero(all_last))
    at_below = all_below + jnp.where(chip == 0, all_last, zero(all_last))
    high, low = zip(*(split(piece) for piece in (all_mine, at_above, all_two, at_below)))
    return update(half, rows, scaled, high, low)


def solution(mesh):
    return jax.shard_map(
        body,
        mesh=mesh,
        in_specs=(P(("pcol", "prow"), None), P("prow", "pcol"), P()),
        out_specs=P("pcol", "prow"),
        check_vma=False,
    )
```

```python
import functools

import jax
import jax.numpy as jnp
from jax import lax
from jax.experimental import pallas as pl
from jax.experimental.pallas import tpu as pltpu
from jax.sharding import PartitionSpec as P

UP_ONE = [(c, c + 2) for c in range(6)]
DOWN_ONE = [(c, c - 2) for c in range(2, 8)]
UP_TWO = [(c, c + 2) for c in range(2, 6)]
DOWN_TWO = [(c, c - 2) for c in range(2, 6)]
UP_END = [(4, 6), (5, 7)]
DOWN_END = [(2, 0), (3, 1)]
SIBLING = [(c, c ^ 1) for c in range(8)]
FAR = [(r, (r + 16) % 32) for r in range(32)]
PLANES = [list(range(16)), list(range(16, 32))]


IN_X = [[4 * q + x for x in range(4)] for q in range(8)]
IN_Y = [[16 * z + 4 * y + x for y in range(4)] for z in range(2) for x in range(4)]
SLOTS, WIDE = 4, 128
CHUNKS, CHAINS = 4, 2


def upper_part(square):
    width = square.shape[0]
    rows = lax.broadcasted_iota(jnp.int32, (width, width), 0)
    cols = lax.broadcasted_iota(jnp.int32, (width, width), 1)
    return jnp.where(cols >= rows, square, jnp.zeros_like(square))


def matmul(left, right, precision=lax.Precision.HIGHEST):
    return jnp.dot(left, right, precision=precision, preferred_element_type=jnp.float32)


def matmul_nt(left, right):
    return lax.dot_general(
        left, right, (((1,), (1,)), ((), ())),
        precision=lax.Precision.HIGH, preferred_element_type=jnp.float32,
    )


def exchange(value, groups):
    return lax.all_to_all(
        value, "prow", split_axis=0, concat_axis=0, tiled=True, axis_index_groups=groups
    )


def gather(value, groups):
    return exchange(jnp.broadcast_to(value, (4, *value.shape)), groups)


def sum_over_plane(values):
    return jnp.sum(gather(jnp.sum(exchange(values, IN_X), axis=0), IN_Y), axis=0)


def far(value):
    return lax.ppermute(value, "prow", FAR)


def turned(parts, start):
    return lax.dynamic_slice_in_dim(jnp.concatenate([parts, parts], axis=0), start % 4, 4, 0)


def split(value):
    high = lax.reduce_precision(value, 8, 7)
    return high.astype(jnp.bfloat16), (value - high).astype(jnp.bfloat16)


def dot_nn(left, right):
    return jnp.dot(left, right, preferred_element_type=jnp.float32)


def dot_nt(left, right):
    return lax.dot_general(
        left, right, (((1,), (1,)), ((), ())), preferred_element_type=jnp.float32
    )


def two_slots(refs, pair):
    return jnp.concatenate([refs[2 * pair][...], refs[2 * pair + 1][...]], axis=0)


def project_kernel(rows_ref, *refs):
    high_refs, low_refs, out_ref = refs[:SLOTS], refs[SLOTS : 2 * SLOTS], refs[-1]

    @pl.when(pl.program_id(0) == 0)
    def _():
        out_ref[...] = jnp.zeros_like(out_ref)

    rows = rows_ref[...].reshape(-1, rows_ref.shape[-1])
    count = rows.shape[0]
    high = rows.astype(jnp.bfloat16)
    low = (rows - high.astype(jnp.float32)).astype(jnp.bfloat16)
    left = jnp.concatenate([high, low], axis=0)
    for pair in range(SLOTS // 2):
        both = dot_nt(left, two_slots(high_refs, pair))
        part = both[:count] + both[count:] + dot_nt(high, two_slots(low_refs, pair))
        out_ref[2 * pair] += part[:, :WIDE]
        out_ref[2 * pair + 1] += part[:, WIDE:]


def project(rows, high, low, start=0, tile=896):
    peers, count, length = rows.shape
    block = pl.BlockSpec((WIDE, tile), lambda i: (0, i + start // tile))
    return pl.pallas_call(
        project_kernel,
        out_shape=jax.ShapeDtypeStruct((SLOTS, peers * count, WIDE), jnp.float32),
        grid=(length // tile,),
        in_specs=[pl.BlockSpec((peers, count, tile), lambda i: (0, 0, i)), *[block] * 8],
        out_specs=pl.BlockSpec((SLOTS, peers * count, WIDE), lambda i: (0, 0, 0)),
        compiler_params=pltpu.CompilerParams(vmem_limit_bytes=60 * 1024 * 1024),
        cost_estimate=pl.CostEstimate(
            flops=6 * peers * count * 512 * length,
            bytes_accessed=length * (512 + peers * count) * 4,
            transcendentals=0,
        ),
    )(rows, *high, *low)


def update_kernel(half_ref, near_ref, scaled_ref, *refs):
    high_refs, low_refs, out_ref = refs[:SLOTS], refs[SLOTS : 2 * SLOTS], refs[-1]
    far_refs = refs[2 * SLOTS : -1]
    per = pl.num_programs(0) // len(far_refs)
    count, mid = out_ref.shape[0], out_ref.shape[0] // 2
    change = None
    for pair in range(SLOTS // 2):
        left = scaled_ref[:, slice(2 * WIDE * pair, 2 * WIDE * (pair + 1))]
        both = dot_nn(left, two_slots(high_refs, pair))
        part = both[:count] + both[count:] + dot_nn(left[:count], two_slots(low_refs, pair))
        change = part if change is None else change + part
    here = pl.multiple_of(half_ref[0] * mid, mid)
    there = pl.multiple_of((1 - half_ref[0]) * mid, mid)
    out_ref[pl.ds(here, mid), :] = near_ref[...].reshape(mid, -1) - change[:mid]
    for chunk, far_ref in enumerate(far_refs):

        @pl.when(pl.program_id(0) // per == chunk)
        def _():
            out_ref[pl.ds(there, mid), :] = far_ref[...].reshape(mid, -1) - change[mid:]


def update(half, near, others, scaled, high, low, tile=896):
    peers, each, length = near.shape
    count = 2 * peers * each
    per = length // tile // len(others)

    def rows(first, last):
        return pl.BlockSpec(
            (peers, each, tile), lambda i, h: (0, 0, jnp.clip(i, first, last) - first)
        )

    block = pl.BlockSpec((WIDE, tile), lambda i, h: (0, i))
    return pl.pallas_call(
        update_kernel,
        out_shape=jax.ShapeDtypeStruct((count, length), jnp.float32),
        grid_spec=pltpu.PrefetchScalarGridSpec(
            num_scalar_prefetch=1,
            grid=(length // tile,),
            in_specs=[
                rows(0, length // tile - 1),
                pl.BlockSpec(scaled.shape, lambda i, h: (0, 0)),
                *[block] * 8,
                *[rows(k * per, k * per + per - 1) for k in range(len(others))],
            ],
            out_specs=pl.BlockSpec((count, tile), lambda i, h: (0, i)),
        ),
        compiler_params=pltpu.CompilerParams(vmem_limit_bytes=60 * 1024 * 1024),
        cost_estimate=pl.CostEstimate(
            flops=6 * count * 512 * length,
            bytes_accessed=length * (512 * 4 + count * 8),
            transcendentals=0,
        ),
    )(half.reshape(1), near, scaled, *high, *low, *others)


def body(eigen_rows, reflectors, tfactors):
    count = eigen_rows.shape[0]
    half = lax.axis_index("prow") // 16
    column = lax.axis_index("pcol")
    chip, core = column // 2, column % 2
    length = reflectors.shape[0]
    mine = reflectors.T

    def send(value, pairs):
        return lax.ppermute(value, "pcol", pairs)

    def both_cores(piece):
        other = send(piece, SIBLING)
        return jnp.concatenate(
            [jnp.where(core == 0, piece, other), jnp.where(core == 0, other, piece)], axis=0
        )

    below = send(mine, UP_ONE)
    above = send(mine, DOWN_ONE)
    blocks = eigen_rows.reshape(count, 32, length).transpose(1, 0, 2)
    leaving = exchange(lax.dynamic_slice_in_dim(blocks, (1 - half) * 16, 16, 0), PLANES)
    near = exchange(lax.dynamic_slice_in_dim(blocks, half * 16, 16, 0), PLANES)
    below_two = send(below, UP_TWO)
    above_two = send(above, DOWN_TWO)
    leaving, below_two, above_two = lax.optimization_barrier((leaving, below_two, above_two))
    span = length // CHUNKS
    others = [leaving[:, :, k * span : (k + 1) * span] for k in range(CHUNKS)]
    for k in range(CHUNKS):
        if k >= CHAINS:
            others[k], others[k - CHAINS] = lax.optimization_barrier(
                (others[k], others[k - CHAINS])
            )
        others[k] = far(others[k])
    below_end = send(below_two, UP_END)
    above_end = send(above_two, DOWN_END)
    two = below_two + above_two
    all_mine, all_below, all_above, all_two = (
        both_cores(piece) for piece in (mine, below, above, two)
    )

    left = jnp.where(chip == 0, two, jnp.where(chip == 3, mine, above))
    right = jnp.where(chip == 0, all_above, jnp.where(chip == 1, all_below, all_two))
    cross = sum_over_plane(matmul_nt(left, right).reshape(4, 16, WIDE))
    cross = gather(cross + far(cross), IN_X).reshape(64, WIDE)
    cross = lax.all_to_all(
        jnp.broadcast_to(cross, (8, *cross.shape)), "pcol", split_axis=0, concat_axis=0, tiled=True
    ).reshape(4, WIDE, WIDE)
    cross = jnp.concatenate(
        [
            jnp.concatenate([cross[1], cross[0]], axis=1),
            jnp.concatenate([cross[2], cross[3]], axis=1),
        ],
        axis=0,
    )

    all_last = both_cores(below_end + above_end)
    zero = jnp.zeros_like(all_last)
    at_above = all_above + jnp.where(chip == 3, all_last, zero)
    at_below = all_below + jnp.where(chip == 0, all_last, zero)
    high, low = zip(*(split(piece) for piece in (all_mine, at_above, all_two, at_below)))

    near_sum = sum_over_plane(project(near, high, low))
    near_elsewhere = far(near_sum)
    early = sum(
        (project(others[k], high, low, k * span) for k in range(1, CHUNKS - 1)),
        project(others[0], high, low),
    )
    last_rows, early, near_sum, near_elsewhere, cross, high, low = lax.optimization_barrier(
        (others[-1], early, near_sum, near_elsewhere, cross, high, low)
    )
    others[-1] = last_rows
    other_sum = sum_over_plane(early + project(last_rows, high, low, length - span))
    near_sum = near_sum + far(other_sum)
    other_sum = other_sum + near_elsewhere
    slots = gather(jnp.concatenate([near_sum, other_sum], axis=0), IN_X)

    projected = turned(slots, 4 - chip)
    first = jnp.concatenate([projected[0], projected[1]], axis=1)
    second = jnp.concatenate([projected[2], projected[3]], axis=1)
    scaled_second = matmul(second, upper_part(tfactors[1]).T)
    scaled_first = matmul(first - matmul(scaled_second, cross), upper_part(tfactors[0]).T)
    scaled = jnp.stack(
        [
            scaled_first[:, :WIDE],
            scaled_first[:, WIDE:],
            scaled_second[:, :WIDE],
            scaled_second[:, WIDE:],
        ]
    )
    scaled = turned(scaled, chip)
    scaled = jnp.concatenate([scaled[j] for j in range(SLOTS)], axis=1)
    scaled = jnp.concatenate(split(scaled), axis=0)
    return update(half, near, others, scaled, high, low)


def solution(mesh):
    return jax.shard_map(
        body,
        mesh=mesh,
        in_specs=(P(("pcol", "prow"), None), P("prow", "pcol"), P()),
        out_specs=P("pcol", "prow"),
        check_vma=False,
    )
```

```python
import functools

import jax
import jax.numpy as jnp
from jax import lax
from jax.experimental import pallas as pl
from jax.experimental.pallas import tpu as pltpu
from jax.sharding import PartitionSpec as P

UP_ONE = [(c, c + 2) for c in range(6)]
DOWN_ONE = [(c, c - 2) for c in range(2, 8)]
UP_TWO = [(c, c + 2) for c in range(2, 6)]
DOWN_TWO = [(c, c - 2) for c in range(2, 6)]
TO_ENDS = [(4, 6), (5, 7), (2, 0), (3, 1)]
SIBLING = [(c, c ^ 1) for c in range(8)]
FAR = [(r, (r + 16) % 32) for r in range(32)]
PLANES = [list(range(16)), list(range(16, 32))]


def along_x(step):
    return [(r, r // 4 * 4 + (r + step) % 4) for r in range(32)]


def along_y(step):
    return [(r, r // 16 * 16 + (r + 4 * step) % 16) for r in range(32)]


def upper_part(square):
    width = square.shape[0]
    rows = lax.broadcasted_iota(jnp.int32, (width, width), 0)
    cols = lax.broadcasted_iota(jnp.int32, (width, width), 1)
    return jnp.where(cols >= rows, square, jnp.zeros_like(square))


def matmul(left, right, precision=lax.Precision.HIGHEST):
    return jnp.dot(left, right, precision=precision, preferred_element_type=jnp.float32)


def matmul_nt(left, right):
    return lax.dot_general(
        left, right, (((1,), (1,)), ((), ())),
        precision=lax.Precision.HIGH, preferred_element_type=jnp.float32,
    )


def sum_over_prow(quarters, block):
    x = lax.axis_index("prow") % 4
    count = quarters.shape[1]

    def send(value, pairs):
        return lax.ppermute(value, "prow", pairs)

    def packed(step):
        part = lax.dynamic_index_in_dim(quarters, (x + step) % 4, 0, keepdims=False)
        return jnp.concatenate([part, block], axis=0)

    total = packed(0)
    for step in (1, 2, 3):
        total = total + send(packed(step), along_x(step))
    total = total + send(total, along_y(1)) + send(total, along_y(2)) + send(total, along_y(3))
    far = send(total, FAR)
    mid = count // 2
    total = total + jnp.concatenate([far[mid:count], far[:mid], far[count:]], axis=0)
    part = total[:count]
    return jnp.stack([part, *(send(part, along_x(4 - step)) for step in (1, 2, 3))]), total[count:]


def turned(parts, start):
    return lax.dynamic_slice_in_dim(jnp.concatenate([parts, parts], axis=0), start % 4, 4, 0)


def split(value):
    high = lax.reduce_precision(value, 8, 7)
    return high.astype(jnp.bfloat16), (value - high).astype(jnp.bfloat16)


def update_kernel(where_ref, rows_ref, scaled_ref, *refs):
    out_ref = refs[-1]
    count, mid = rows_ref.shape[0], rows_ref.shape[0] // 2
    mine, above, two, below, last = (
        jnp.concatenate([refs[j][...], refs[j + 1][...]], axis=0) for j in range(0, 10, 2)
    )
    above = jnp.where(where_ref[2] == 0, last, above)
    below = jnp.where(where_ref[3] == 0, last, below)
    dot = functools.partial(jnp.dot, preferred_element_type=jnp.float32)
    change = None
    for pair, slots in enumerate(((mine, above), (two, below))):
        vectors = jnp.concatenate(slots, axis=0)
        high = vectors.astype(jnp.bfloat16)
        low = (vectors - high.astype(jnp.float32)).astype(jnp.bfloat16)
        left = scaled_ref[:, slice(256 * pair, 256 * pair + 256)]
        both = dot(left, high)
        part = both[:count] + both[count:] + dot(left[:count], low)
        change = part if change is None else change + part
    result = rows_ref[...] - change
    place = pl.multiple_of(where_ref[0] * mid, mid)
    other = pl.multiple_of((1 - where_ref[0]) * mid, mid)
    out_ref[pl.ds(place, mid), :] = result[:mid]
    out_ref[pl.ds(other, mid), :] = result[mid:]


def update(half, chip, rows, scaled, pieces, tile=1024):
    count, length = rows.shape
    where = jnp.stack(
        [half, chip, (chip != 3) * 1, (chip != 0) * 1, ((chip == 0) | (chip == 3)) * 1]
    ).astype(jnp.int32)
    streams = (None, 2, None, 3, 4)

    def piece(flag):
        if flag is None:
            return pl.BlockSpec((64, tile), lambda i, w: (0, i))
        return pl.BlockSpec((64, tile), lambda i, w: (0, i * w[flag]))

    return pl.pallas_call(
        update_kernel,
        out_shape=jax.ShapeDtypeStruct(rows.shape, jnp.float32),
        grid_spec=pltpu.PrefetchScalarGridSpec(
            num_scalar_prefetch=1,
            grid=(length // tile,),
            in_specs=[
                pl.BlockSpec((count, tile), lambda i, w: (0, i)),
                pl.BlockSpec(scaled.shape, lambda i, w: (0, 0)),
                *[piece(flag) for flag in streams for _ in range(2)],
            ],
            out_specs=pl.BlockSpec((count, tile), lambda i, w: (0, i)),
        ),
        compiler_params=pltpu.CompilerParams(vmem_limit_bytes=60 * 1024 * 1024),
        cost_estimate=pl.CostEstimate(
            flops=6 * count * 512 * length,
            bytes_accessed=length * (count * 8 + 512 * 4),
            transcendentals=0,
        ),
    )(where, rows, scaled, *pieces)


def body(eigen_rows, reflectors, tfactors):
    count = eigen_rows.shape[0]
    prow = lax.axis_index("prow")
    x, half = prow % 4, prow // 16
    column = lax.axis_index("pcol")
    chip, core = column // 2, column % 2
    length = reflectors.shape[0]
    mine = reflectors.T

    def send(value, pairs):
        return lax.ppermute(value, "pcol", pairs)

    def ordered(piece, other, axis):
        return jnp.concatenate(
            [jnp.where(core == 0, piece, other), jnp.where(core == 0, other, piece)], axis=axis
        )

    blocks = eigen_rows.reshape(count, 32, length).transpose(1, 0, 2)
    leaving = lax.dynamic_slice_in_dim(blocks, (1 - half) * 16, 16, 0)
    staying = lax.dynamic_slice_in_dim(blocks, half * 16, 16, 0)
    mine, leaving = lax.optimization_barrier((mine, leaving))
    arriving = lax.ppermute(leaving, "prow", FAR)
    below = send(mine, UP_ONE)
    above = send(mine, DOWN_ONE)

    def over_plane(value):
        value = lax.all_to_all(
            value, "prow", split_axis=0, concat_axis=0, tiled=True, axis_index_groups=PLANES
        )
        return value.reshape(16 * count, length)

    staying = over_plane(staying)
    below_two = send(below, UP_TWO)
    above_two = send(above, DOWN_TWO)
    arriving = over_plane(arriving)
    arriving, below_two, above_two = lax.optimization_barrier((arriving, below_two, above_two))
    last = send(jnp.where(chip == 2, below_two, above_two), TO_ENDS)
    rows = jnp.concatenate([staying, arriving], axis=0)
    two = below_two + above_two

    pieces = (mine, above, two, below)
    swapped = [send(piece, SIBLING) for piece in pieces]
    all_mine, all_above, all_two, all_below = (
        ordered(piece, other, 0) for piece, other in zip(pieces, swapped)
    )

    left = jnp.where(chip == 0, two, jnp.where(chip == 3, mine, above))
    right = jnp.where(chip == 0, all_above, jnp.where(chip == 1, all_below, all_two))
    cross = matmul_nt(left, right)
    on_mine, on_two = matmul_nt(rows, all_mine), matmul_nt(rows, all_two)
    on_above, on_below = matmul_nt(rows, all_above), matmul_nt(rows, all_below)
    last, cross, on_mine, on_two, on_above, on_below = lax.optimization_barrier(
        (last, cross, on_mine, on_two, on_above, on_below)
    )

    last_other = send(last, SIBLING)
    zero = jnp.zeros_like
    last_other, on_last = lax.optimization_barrier((last_other, matmul_nt(rows, last)))
    on_last = ordered(on_last, matmul_nt(rows, last_other), 1)
    slots = jnp.stack(
        [
            on_mine,
            on_above + jnp.where(chip == 3, on_last, zero(on_last)),
            on_two,
            on_below + jnp.where(chip == 0, on_last, zero(on_last)),
        ]
    )
    projected, cross = sum_over_prow(slots, cross)
    cross = lax.all_to_all(
        jnp.broadcast_to(cross, (8, *cross.shape)), "pcol", split_axis=0, concat_axis=0, tiled=True
    ).reshape(4, 128, 128)
    cross = jnp.concatenate(
        [
            jnp.concatenate([cross[1], cross[0]], axis=1),
            jnp.concatenate([cross[2], cross[3]], axis=1),
        ],
        axis=0,
    )
    projected = turned(projected, 8 - chip - x)
    first = jnp.concatenate([projected[0], projected[1]], axis=1)
    second = jnp.concatenate([projected[2], projected[3]], axis=1)
    scaled_second = matmul(second, upper_part(tfactors[1]).T)
    scaled_first = matmul(first - matmul(scaled_second, cross), upper_part(tfactors[0]).T)
    scaled = jnp.stack(
        [scaled_first[:, :128], scaled_first[:, 128:], scaled_second[:, :128], scaled_second[:, 128:]]
    )
    scaled = turned(scaled, chip)
    scaled = jnp.where(core == 0, scaled, jnp.roll(scaled, 64, axis=2))
    scaled = jnp.concatenate([scaled[j] for j in range(4)], axis=1)
    scaled = jnp.concatenate(split(scaled), axis=0)

    pieces, swapped = (*pieces, last), (*swapped, last_other)
    return update(half, chip, rows, scaled, [v for pair in zip(pieces, swapped) for v in pair])


def solution(mesh):
    return jax.shard_map(
        body,
        mesh=mesh,
        in_specs=(P(("pcol", "prow"), None), P("prow", "pcol"), P()),
        out_specs=P("pcol", "prow"),
        check_vma=False,
    )
```

```python
import functools

import jax
import jax.numpy as jnp
from jax import lax
from jax.experimental import pallas as pl
from jax.experimental.pallas import tpu as pltpu
from jax.sharding import PartitionSpec as P

UP_ONE = [(c, c + 2) for c in range(6)]
DOWN_ONE = [(c, c - 2) for c in range(2, 8)]
UP_TWO = [(c, c + 2) for c in range(2, 6)]
DOWN_TWO = [(c, c - 2) for c in range(2, 6)]
TO_ENDS = [(4, 6), (5, 7), (2, 0), (3, 1)]
SIBLING = [(c, c ^ 1) for c in range(8)]
FAR = [(r, (r + 16) % 32) for r in range(32)]
PLANES = [list(range(16)), list(range(16, 32))]


def along_x(step):
    return [(r, r // 4 * 4 + (r + step) % 4) for r in range(32)]


def along_y(step):
    return [(r, r // 16 * 16 + (r + 4 * step) % 16) for r in range(32)]


def upper_part(square):
    width = square.shape[0]
    rows = lax.broadcasted_iota(jnp.int32, (width, width), 0)
    cols = lax.broadcasted_iota(jnp.int32, (width, width), 1)
    return jnp.where(cols >= rows, square, jnp.zeros_like(square))


def matmul(left, right, precision=lax.Precision.HIGHEST):
    return jnp.dot(left, right, precision=precision, preferred_element_type=jnp.float32)


def matmul_nt(left, right):
    return lax.dot_general(
        left, right, (((1,), (1,)), ((), ())),
        precision=lax.Precision.HIGH, preferred_element_type=jnp.float32,
    )


def sum_over_prow(quarters):
    x = lax.axis_index("prow") % 4

    def send(value, pairs):
        return lax.ppermute(value, "prow", pairs)

    def quarter(step):
        return lax.dynamic_index_in_dim(quarters, (x + step) % 4, 0, keepdims=False)

    total = quarter(0)
    for step in (1, 2, 3):
        total = total + send(quarter(step), along_x(step))
    total = total + send(total, along_y(1)) + send(total, along_y(2)) + send(total, along_y(3))
    far = send(total, FAR)
    total = total + jnp.concatenate([far[64:128], far[:64], far[128:]], axis=0)
    return jnp.stack([total, *(send(total, along_x(4 - step)) for step in (1, 2, 3))])


def turned(parts, start):
    return lax.dynamic_slice_in_dim(jnp.concatenate([parts, parts], axis=0), start % 4, 4, 0)


def split(value):
    high = lax.reduce_precision(value, 8, 7)
    return high.astype(jnp.bfloat16), (value - high).astype(jnp.bfloat16)


def update_kernel(where_ref, rows_ref, scaled_ref, *refs):
    out_ref = refs[-1]
    count, mid = rows_ref.shape[0], rows_ref.shape[0] // 2
    mine, above, two, below, last = (
        jnp.concatenate([refs[j][...], refs[j + 1][...]], axis=0) for j in range(0, 10, 2)
    )
    above = jnp.where(where_ref[2] == 0, last, above)
    below = jnp.where(where_ref[3] == 0, last, below)
    dot = functools.partial(jnp.dot, preferred_element_type=jnp.float32)
    change = None
    for pair, slots in enumerate(((mine, above), (two, below))):
        vectors = jnp.concatenate(slots, axis=0)
        high = vectors.astype(jnp.bfloat16)
        low = (vectors - high.astype(jnp.float32)).astype(jnp.bfloat16)
        left = scaled_ref[:, slice(256 * pair, 256 * pair + 256)]
        both = dot(left, high)
        part = both[:count] + both[count:] + dot(left[:count], low)
        change = part if change is None else change + part
    result = rows_ref[...] - change
    place = pl.multiple_of(where_ref[0] * mid, mid)
    other = pl.multiple_of((1 - where_ref[0]) * mid, mid)
    out_ref[pl.ds(place, mid), :] = result[:mid]
    out_ref[pl.ds(other, mid), :] = result[mid:]


def update(half, chip, rows, scaled, pieces, tile=1024):
    count, length = rows.shape
    where = jnp.stack(
        [half, chip, (chip != 3) * 1, (chip != 0) * 1, ((chip == 0) | (chip == 3)) * 1]
    ).astype(jnp.int32)
    streams = (None, 2, None, 3, 4)

    def piece(flag):
        if flag is None:
            return pl.BlockSpec((64, tile), lambda i, w: (0, i))
        return pl.BlockSpec((64, tile), lambda i, w: (0, i * w[flag]))

    return pl.pallas_call(
        update_kernel,
        out_shape=jax.ShapeDtypeStruct(rows.shape, jnp.float32),
        grid_spec=pltpu.PrefetchScalarGridSpec(
            num_scalar_prefetch=1,
            grid=(length // tile,),
            in_specs=[
                pl.BlockSpec((count, tile), lambda i, w: (0, i)),
                pl.BlockSpec(scaled.shape, lambda i, w: (0, 0)),
                *[piece(flag) for flag in streams for _ in range(2)],
            ],
            out_specs=pl.BlockSpec((count, tile), lambda i, w: (0, i)),
        ),
        compiler_params=pltpu.CompilerParams(vmem_limit_bytes=60 * 1024 * 1024),
        cost_estimate=pl.CostEstimate(
            flops=6 * count * 512 * length,
            bytes_accessed=length * (count * 8 + 512 * 4),
            transcendentals=0,
        ),
    )(where, rows, scaled, *pieces)


def body(eigen_rows, reflectors, tfactors):
    count = eigen_rows.shape[0]
    prow = lax.axis_index("prow")
    x, half = prow % 4, prow // 16
    column = lax.axis_index("pcol")
    chip, core = column // 2, column % 2
    length = reflectors.shape[0]
    mine = reflectors.T

    def send(value, pairs):
        return lax.ppermute(value, "pcol", pairs)

    def ordered(piece, other, axis):
        return jnp.concatenate(
            [jnp.where(core == 0, piece, other), jnp.where(core == 0, other, piece)], axis=axis
        )

    blocks = eigen_rows.reshape(count, 32, length).transpose(1, 0, 2)
    leaving = lax.dynamic_slice_in_dim(blocks, (1 - half) * 16, 16, 0)
    staying = lax.dynamic_slice_in_dim(blocks, half * 16, 16, 0)
    mine, leaving = lax.optimization_barrier((mine, leaving))
    arriving = lax.ppermute(leaving, "prow", FAR)
    below = send(mine, UP_ONE)
    above = send(mine, DOWN_ONE)

    def over_plane(value):
        value = lax.all_to_all(
            value, "prow", split_axis=0, concat_axis=0, tiled=True, axis_index_groups=PLANES
        )
        return value.reshape(16 * count, length)

    staying = over_plane(staying)
    below_two = send(below, UP_TWO)
    above_two = send(above, DOWN_TWO)
    arriving = over_plane(arriving)
    arriving, _, _ = lax.optimization_barrier((arriving, below_two, above_two))
    last = send(jnp.where(chip == 2, below_two, above_two), TO_ENDS)
    rows = jnp.concatenate([staying, arriving], axis=0)
    two = below_two + above_two

    pieces = (mine, above, two, below)
    swapped = [send(piece, SIBLING) for piece in pieces]
    all_mine, all_above, all_two, all_below = (
        ordered(piece, other, 0) for piece, other in zip(pieces, swapped)
    )

    left = jnp.where(chip == 0, two, jnp.where(chip == 3, mine, above))
    right = jnp.where(chip == 0, all_above, jnp.where(chip == 1, all_below, all_two))
    cross = lax.all_to_all(
        jnp.broadcast_to(matmul_nt(left, right), (8, 64, 128)),
        "pcol", split_axis=0, concat_axis=0, tiled=True,
    ).reshape(4, 128, 128)
    cross = jnp.stack([cross[1], cross[0], cross[2], cross[3]])
    on_mine, on_two = matmul_nt(rows, all_mine), matmul_nt(rows, all_two)
    on_above, on_below = matmul_nt(rows, all_above), matmul_nt(rows, all_below)
    last, cross, on_mine, on_two, on_above, on_below = lax.optimization_barrier(
        (last, cross, on_mine, on_two, on_above, on_below)
    )
    last_other = send(last, SIBLING)
    on_last = matmul_nt(rows, jnp.concatenate([last, last_other], axis=0))
    on_last = jnp.where(core == 0, on_last, jnp.roll(on_last, 64, axis=1))
    zero = jnp.zeros_like(on_last)
    slots = jnp.stack(
        [
            on_mine,
            on_above + jnp.where(chip == 3, on_last, zero),
            on_two,
            on_below + jnp.where(chip == 0, on_last, zero),
        ]
    )
    summed = sum_over_prow(jnp.concatenate([slots, cross], axis=1))
    cross = turned(summed[:, 128:], 4 - x)
    cross = jnp.concatenate(
        [
            jnp.concatenate([cross[0], cross[1]], axis=1),
            jnp.concatenate([cross[2], cross[3]], axis=1),
        ],
        axis=0,
    )
    projected = turned(summed[:, :128], 8 - chip - x)
    first = jnp.concatenate([projected[0], projected[1]], axis=1)
    second = jnp.concatenate([projected[2], projected[3]], axis=1)
    scaled_second = matmul(second, upper_part(tfactors[1]).T)
    scaled_first = matmul(first - matmul(scaled_second, cross), upper_part(tfactors[0]).T)
    scaled = jnp.stack(
        [scaled_first[:, :128], scaled_first[:, 128:], scaled_second[:, :128], scaled_second[:, 128:]]
    )
    scaled = turned(scaled, chip)
    scaled = jnp.where(core == 0, scaled, jnp.roll(scaled, 64, axis=2))
    scaled = jnp.concatenate([scaled[j] for j in range(4)], axis=1)
    scaled = jnp.concatenate(split(scaled), axis=0)

    pieces, swapped = (*pieces, last), (*swapped, last_other)
    return update(half, chip, rows, scaled, [v for pair in zip(pieces, swapped) for v in pair])


def solution(mesh):
    return jax.shard_map(
        body,
        mesh=mesh,
        in_specs=(P(("pcol", "prow"), None), P("prow", "pcol"), P()),
        out_specs=P("pcol", "prow"),
        check_vma=False,
    )
```

```python
import functools

import jax
import jax.numpy as jnp
from jax import lax
from jax.experimental import pallas as pl
from jax.experimental.pallas import tpu as pltpu
from jax.sharding import PartitionSpec as P

UP_ONE = [(c, c + 2) for c in range(6)]
DOWN_ONE = [(c, c - 2) for c in range(2, 8)]
UP_TWO = [(c, c + 2) for c in range(2, 6)]
DOWN_TWO = [(c, c - 2) for c in range(2, 6)]
TO_ENDS = [(4, 6), (5, 7), (2, 0), (3, 1)]
SIBLING = [(c, c ^ 1) for c in range(8)]
FAR = [(r, (r + 16) % 32) for r in range(32)]
PLANES = [list(range(16)), list(range(16, 32))]


def along_x(step):
    return [(r, r // 4 * 4 + (r + step) % 4) for r in range(32)]


def along_y(step):
    return [(r, r // 16 * 16 + (r + 4 * step) % 16) for r in range(32)]


def upper_part(square):
    width = square.shape[0]
    rows = lax.broadcasted_iota(jnp.int32, (width, width), 0)
    cols = lax.broadcasted_iota(jnp.int32, (width, width), 1)
    return jnp.where(cols >= rows, square, jnp.zeros_like(square))


def matmul(left, right, precision=lax.Precision.HIGHEST):
    return jnp.dot(left, right, precision=precision, preferred_element_type=jnp.float32)


def matmul_nt(left, right):
    return lax.dot_general(
        left, right, (((1,), (1,)), ((), ())),
        precision=lax.Precision.HIGH, preferred_element_type=jnp.float32,
    )


def sum_over_prow(quarters):
    x = lax.axis_index("prow") % 4

    def send(value, pairs):
        return lax.ppermute(value, "prow", pairs)

    def quarter(step):
        return lax.dynamic_index_in_dim(quarters, (x + step) % 4, 0, keepdims=False)

    total = quarter(0)
    for step in (1, 2, 3):
        total = total + send(quarter(step), along_x(step))
    total = total + send(total, along_y(1)) + send(total, along_y(2)) + send(total, along_y(3))
    far = send(total, FAR)
    total = total + jnp.concatenate([far[64:128], far[:64], far[128:]], axis=0)
    return jnp.stack([total, *(send(total, along_x(4 - step)) for step in (1, 2, 3))])


def turned(parts, start):
    return lax.dynamic_slice_in_dim(jnp.concatenate([parts, parts], axis=0), start % 4, 4, 0)


def split(value):
    high = lax.reduce_precision(value, 8, 7)
    return high.astype(jnp.bfloat16), (value - high).astype(jnp.bfloat16)


def update_kernel(where_ref, rows_ref, scaled_ref, *refs):
    out_ref = refs[-1]
    count, mid = rows_ref.shape[0], rows_ref.shape[0] // 2
    mine, above, two, below, last = (
        jnp.concatenate([refs[j][...], refs[j + 1][...]], axis=0) for j in range(0, 10, 2)
    )
    above = jnp.where(where_ref[2] == 0, last, above)
    below = jnp.where(where_ref[3] == 0, last, below)
    dot = functools.partial(jnp.dot, preferred_element_type=jnp.float32)
    change = None
    for pair, slots in enumerate(((mine, above), (two, below))):
        vectors = jnp.concatenate(slots, axis=0)
        high = vectors.astype(jnp.bfloat16)
        low = (vectors - high.astype(jnp.float32)).astype(jnp.bfloat16)
        left = scaled_ref[:, slice(256 * pair, 256 * pair + 256)]
        both = dot(left, high)
        part = both[:count] + both[count:] + dot(left[:count], low)
        change = part if change is None else change + part
    result = rows_ref[...] - change
    place = pl.multiple_of(where_ref[0] * mid, mid)
    other = pl.multiple_of((1 - where_ref[0]) * mid, mid)
    out_ref[pl.ds(place, mid), :] = result[:mid]
    out_ref[pl.ds(other, mid), :] = result[mid:]


def update(half, chip, rows, scaled, pieces, tile=1792):
    count, length = rows.shape
    where = jnp.stack(
        [half, chip, (chip != 3) * 1, (chip != 0) * 1, ((chip == 0) | (chip == 3)) * 1]
    ).astype(jnp.int32)
    streams = (None, 2, None, 3, 4)

    def piece(flag):
        if flag is None:
            return pl.BlockSpec((64, tile), lambda i, w: (0, i))
        return pl.BlockSpec((64, tile), lambda i, w: (0, i * w[flag]))

    return pl.pallas_call(
        update_kernel,
        out_shape=jax.ShapeDtypeStruct(rows.shape, jnp.float32),
        grid_spec=pltpu.PrefetchScalarGridSpec(
            num_scalar_prefetch=1,
            grid=(length // tile,),
            in_specs=[
                pl.BlockSpec((count, tile), lambda i, w: (0, i)),
                pl.BlockSpec(scaled.shape, lambda i, w: (0, 0)),
                *[piece(flag) for flag in streams for _ in range(2)],
            ],
            out_specs=pl.BlockSpec((count, tile), lambda i, w: (0, i)),
        ),
        compiler_params=pltpu.CompilerParams(vmem_limit_bytes=60 * 1024 * 1024),
        cost_estimate=pl.CostEstimate(
            flops=6 * count * 512 * length,
            bytes_accessed=length * (count * 8 + 512 * 4),
            transcendentals=0,
        ),
    )(where, rows, scaled, *pieces)


def body(eigen_rows, reflectors, tfactors):
    count = eigen_rows.shape[0]
    prow = lax.axis_index("prow")
    x, half = prow % 4, prow // 16
    column = lax.axis_index("pcol")
    chip, core = column // 2, column % 2
    length = reflectors.shape[0]
    mine = reflectors.T

    def send(value, pairs):
        return lax.ppermute(value, "pcol", pairs)

    def ordered(piece, other, axis):
        return jnp.concatenate(
            [jnp.where(core == 0, piece, other), jnp.where(core == 0, other, piece)], axis=axis
        )

    blocks = eigen_rows.reshape(count, 32, length).transpose(1, 0, 2)
    leaving = lax.dynamic_slice_in_dim(blocks, (1 - half) * 16, 16, 0)
    staying = lax.dynamic_slice_in_dim(blocks, half * 16, 16, 0)
    mine, leaving = lax.optimization_barrier((mine, leaving))
    arriving = lax.ppermute(leaving, "prow", FAR)
    below = send(mine, UP_ONE)
    above = send(mine, DOWN_ONE)

    def over_plane(value):
        value = lax.all_to_all(
            value, "prow", split_axis=0, concat_axis=0, tiled=True, axis_index_groups=PLANES
        )
        return value.reshape(16 * count, length)

    staying = over_plane(staying)
    below_two = send(below, UP_TWO)
    above_two = send(above, DOWN_TWO)
    arriving = over_plane(arriving)
    arriving, _, _ = lax.optimization_barrier((arriving, below_two, above_two))
    last = send(jnp.where(chip == 2, below_two, above_two), TO_ENDS)
    rows = jnp.concatenate([staying, arriving], axis=0)
    two = below_two + above_two

    pieces = (mine, above, two, below)
    swapped = [send(piece, SIBLING) for piece in pieces]
    all_mine, all_above, all_two, all_below = (
        ordered(piece, other, 0) for piece, other in zip(pieces, swapped)
    )

    left = jnp.where(chip == 0, two, jnp.where(chip == 3, mine, above))
    right = jnp.where(chip == 0, all_above, jnp.where(chip == 1, all_below, all_two))
    cross = matmul_nt(left, right)
    cross = ordered(cross, send(cross, SIBLING), 0)
    cross = turned(
        jnp.stack(
            [cross]
            + [send(cross, [(c, (c + 2 * (4 - step)) % 8) for c in range(8)]) for step in (1, 2, 3)]
        ),
        4 - chip,
    )
    cross = jnp.stack([cross[1], cross[0], cross[2], cross[3]])
    on_mine, on_two = matmul_nt(rows, all_mine), matmul_nt(rows, all_two)
    on_above, on_below = matmul_nt(rows, all_above), matmul_nt(rows, all_below)
    last, cross, on_mine, on_two, on_above, on_below = lax.optimization_barrier(
        (last, cross, on_mine, on_two, on_above, on_below)
    )
    last_other = send(last, SIBLING)
    both = lax.optimization_barrier(jnp.concatenate([last, last_other], axis=0))
    on_last = matmul_nt(rows, both)
    on_last = jnp.where(core == 0, on_last, jnp.roll(on_last, 64, axis=1))
    zero = jnp.zeros_like(on_last)
    slots = jnp.stack(
        [
            on_mine,
            on_above + jnp.where(chip == 3, on_last, zero),
            on_two,
            on_below + jnp.where(chip == 0, on_last, zero),
        ]
    )
    summed = sum_over_prow(jnp.concatenate([slots, cross], axis=1))
    cross = turned(summed[:, 128:], 4 - x)
    cross = jnp.concatenate(
        [
            jnp.concatenate([cross[0], cross[1]], axis=1),
            jnp.concatenate([cross[2], cross[3]], axis=1),
        ],
        axis=0,
    )
    projected = turned(summed[:, :128], 8 - chip - x)
    first = jnp.concatenate([projected[0], projected[1]], axis=1)
    second = jnp.concatenate([projected[2], projected[3]], axis=1)
    scaled_second = matmul(second, upper_part(tfactors[1]).T)
    scaled_first = matmul(first - matmul(scaled_second, cross), upper_part(tfactors[0]).T)
    scaled = jnp.stack(
        [scaled_first[:, :128], scaled_first[:, 128:], scaled_second[:, :128], scaled_second[:, 128:]]
    )
    scaled = turned(scaled, chip)
    scaled = jnp.where(core == 0, scaled, jnp.roll(scaled, 64, axis=2))
    scaled = jnp.concatenate([scaled[j] for j in range(4)], axis=1)
    scaled = jnp.concatenate(split(scaled), axis=0)

    pieces, swapped = (*pieces, last), (*swapped, last_other)
    return update(half, chip, rows, scaled, [v for pair in zip(pieces, swapped) for v in pair])


def solution(mesh):
    return jax.shard_map(
        body,
        mesh=mesh,
        in_specs=(P(("pcol", "prow"), None), P("prow", "pcol"), P()),
        out_specs=P("pcol", "prow"),
        check_vma=False,
    )
```

```python
import functools

import jax
import jax.numpy as jnp
from jax import lax
from jax.experimental import pallas as pl
from jax.experimental.pallas import tpu as pltpu
from jax.sharding import PartitionSpec as P

UP_ONE = [(c, c + 2) for c in range(6)]
DOWN_ONE = [(c, c - 2) for c in range(2, 8)]
UP_TWO = [(c, c + 2) for c in range(2, 6)]
DOWN_TWO = [(c, c - 2) for c in range(2, 6)]
TO_ENDS = [(4, 6), (5, 7), (2, 0), (3, 1)]
SIBLING = [(c, c ^ 1) for c in range(8)]
FAR = [(r, (r + 16) % 32) for r in range(32)]
PLANES = [list(range(16)), list(range(16, 32))]


def along_x(step):
    return [(r, r // 4 * 4 + (r + step) % 4) for r in range(32)]


def along_y(step):
    return [(r, r // 16 * 16 + (r + 4 * step) % 16) for r in range(32)]


def upper_part(square):
    width = square.shape[0]
    rows = lax.broadcasted_iota(jnp.int32, (width, width), 0)
    cols = lax.broadcasted_iota(jnp.int32, (width, width), 1)
    return jnp.where(cols >= rows, square, jnp.zeros_like(square))


def matmul(left, right, precision=lax.Precision.HIGHEST):
    return jnp.dot(left, right, precision=precision, preferred_element_type=jnp.float32)


def matmul_nt(left, right):
    return lax.dot_general(
        left, right, (((1,), (1,)), ((), ())),
        precision=lax.Precision.HIGH, preferred_element_type=jnp.float32,
    )


def sum_over_prow(quarters, block):
    x = lax.axis_index("prow") % 4
    count = quarters.shape[1]

    def send(value, pairs):
        return lax.ppermute(value, "prow", pairs)

    def packed(step):
        part = lax.dynamic_index_in_dim(quarters, (x + step) % 4, 0, keepdims=False)
        return jnp.concatenate([part, block], axis=0)

    total = packed(0)
    for step in (1, 2, 3):
        total = total + send(packed(step), along_x(step))
    total = total + send(total, along_y(1)) + send(total, along_y(2)) + send(total, along_y(3))
    far = send(total, FAR)
    mid = count // 2
    total = total + jnp.concatenate([far[mid:count], far[:mid], far[count:]], axis=0)
    part = total[:count]
    return jnp.stack([part, *(send(part, along_x(4 - step)) for step in (1, 2, 3))]), total[count:]


def turned(parts, start):
    return lax.dynamic_slice_in_dim(jnp.concatenate([parts, parts], axis=0), start % 4, 4, 0)


def split(value):
    high = lax.reduce_precision(value, 8, 7)
    return high.astype(jnp.bfloat16), (value - high).astype(jnp.bfloat16)


def update_kernel(where_ref, rows_ref, scaled_ref, *refs):
    out_ref = refs[-1]
    count, mid = rows_ref.shape[0], rows_ref.shape[0] // 2
    mine, above, two, below, last = (
        jnp.concatenate([refs[j][...], refs[j + 1][...]], axis=0) for j in range(0, 10, 2)
    )
    above = jnp.where(where_ref[2] == 0, last, above)
    below = jnp.where(where_ref[3] == 0, last, below)
    dot = functools.partial(jnp.dot, preferred_element_type=jnp.float32)
    change = None
    for pair, slots in enumerate(((mine, above), (two, below))):
        vectors = jnp.concatenate(slots, axis=0)
        high = vectors.astype(jnp.bfloat16)
        low = (vectors - high.astype(jnp.float32)).astype(jnp.bfloat16)
        left = scaled_ref[:, slice(256 * pair, 256 * pair + 256)]
        both = dot(left, high)
        part = both[:count] + both[count:] + dot(left[:count], low)
        change = part if change is None else change + part
    result = rows_ref[...] - change
    place = pl.multiple_of(where_ref[0] * mid, mid)
    other = pl.multiple_of((1 - where_ref[0]) * mid, mid)
    out_ref[pl.ds(place, mid), :] = result[:mid]
    out_ref[pl.ds(other, mid), :] = result[mid:]


def update(half, chip, rows, scaled, pieces, tile=1792):
    count, length = rows.shape
    where = jnp.stack(
        [half, chip, (chip != 3) * 1, (chip != 0) * 1, ((chip == 0) | (chip == 3)) * 1]
    ).astype(jnp.int32)
    streams = (None, 2, None, 3, 4)

    def piece(flag):
        if flag is None:
            return pl.BlockSpec((64, tile), lambda i, w: (0, i))
        return pl.BlockSpec((64, tile), lambda i, w: (0, i * w[flag]))

    return pl.pallas_call(
        update_kernel,
        out_shape=jax.ShapeDtypeStruct(rows.shape, jnp.float32),
        grid_spec=pltpu.PrefetchScalarGridSpec(
            num_scalar_prefetch=1,
            grid=(length // tile,),
            in_specs=[
                pl.BlockSpec((count, tile), lambda i, w: (0, i)),
                pl.BlockSpec(scaled.shape, lambda i, w: (0, 0)),
                *[piece(flag) for flag in streams for _ in range(2)],
            ],
            out_specs=pl.BlockSpec((count, tile), lambda i, w: (0, i)),
        ),
        compiler_params=pltpu.CompilerParams(vmem_limit_bytes=60 * 1024 * 1024),
        cost_estimate=pl.CostEstimate(
            flops=6 * count * 512 * length,
            bytes_accessed=length * (count * 8 + 512 * 4),
            transcendentals=0,
        ),
    )(where, rows, scaled, *pieces)


def body(eigen_rows, reflectors, tfactors):
    count = eigen_rows.shape[0]
    prow = lax.axis_index("prow")
    x, half = prow % 4, prow // 16
    column = lax.axis_index("pcol")
    chip, core = column // 2, column % 2
    length = reflectors.shape[0]
    mine = reflectors.T

    def send(value, pairs):
        return lax.ppermute(value, "pcol", pairs)

    def ordered(piece, other, axis):
        return jnp.concatenate(
            [jnp.where(core == 0, piece, other), jnp.where(core == 0, other, piece)], axis=axis
        )

    blocks = eigen_rows.reshape(count, 32, length).transpose(1, 0, 2)
    leaving = lax.dynamic_slice_in_dim(blocks, (1 - half) * 16, 16, 0)
    staying = lax.dynamic_slice_in_dim(blocks, half * 16, 16, 0)
    mine, leaving = lax.optimization_barrier((mine, leaving))
    arriving = lax.ppermute(leaving, "prow", FAR)
    below = send(mine, UP_ONE)
    above = send(mine, DOWN_ONE)

    def over_plane(value):
        value = lax.all_to_all(
            value, "prow", split_axis=0, concat_axis=0, tiled=True, axis_index_groups=PLANES
        )
        return value.reshape(16 * count, length)

    staying = over_plane(staying)
    below_two = send(below, UP_TWO)
    above_two = send(above, DOWN_TWO)
    arriving = over_plane(arriving)
    last = send(jnp.where(chip == 2, below_two, above_two), TO_ENDS)
    rows = jnp.concatenate([staying, arriving], axis=0)
    two = below_two + above_two

    pieces = (mine, above, two, below)
    swapped = [send(piece, SIBLING) for piece in pieces]
    all_mine, all_above, all_two, all_below = (
        ordered(piece, other, 0) for piece, other in zip(pieces, swapped)
    )

    left = jnp.where(chip == 0, two, jnp.where(chip == 3, mine, above))
    right = jnp.where(chip == 0, all_above, jnp.where(chip == 1, all_below, all_two))
    cross = matmul_nt(left, right)
    on_mine, on_two = matmul_nt(rows, all_mine), matmul_nt(rows, all_two)
    on_above, on_below = matmul_nt(rows, all_above), matmul_nt(rows, all_below)
    last, cross, on_mine, on_two, on_above, on_below = lax.optimization_barrier(
        (last, cross, on_mine, on_two, on_above, on_below)
    )
    last_other = send(last, SIBLING)
    both = lax.optimization_barrier(jnp.concatenate([last, last_other], axis=0))
    on_last = matmul_nt(rows, both)
    on_last = jnp.where(core == 0, on_last, jnp.roll(on_last, 64, axis=1))
    zero = jnp.zeros_like(on_last)
    slots = jnp.stack(
        [
            on_mine,
            on_above + jnp.where(chip == 3, on_last, zero),
            on_two,
            on_below + jnp.where(chip == 0, on_last, zero),
        ]
    )
    projected, cross = sum_over_prow(slots, cross)
    cross = ordered(cross, send(cross, SIBLING), 0)
    cross = turned(
        jnp.stack(
            [cross]
            + [send(cross, [(c, (c + 2 * (4 - step)) % 8) for c in range(8)]) for step in (1, 2, 3)]
        ),
        4 - chip,
    )
    cross = jnp.concatenate(
        [
            jnp.concatenate([cross[1], cross[0]], axis=1),
            jnp.concatenate([cross[2], cross[3]], axis=1),
        ],
        axis=0,
    )
    projected = turned(projected, 8 - chip - x)
    first = jnp.concatenate([projected[0], projected[1]], axis=1)
    second = jnp.concatenate([projected[2], projected[3]], axis=1)
    scaled_second = matmul(second, upper_part(tfactors[1]).T)
    scaled_first = matmul(first - matmul(scaled_second, cross), upper_part(tfactors[0]).T)
    scaled = jnp.stack(
        [scaled_first[:, :128], scaled_first[:, 128:], scaled_second[:, :128], scaled_second[:, 128:]]
    )
    scaled = turned(scaled, chip)
    scaled = jnp.where(core == 0, scaled, jnp.roll(scaled, 64, axis=2))
    scaled = jnp.concatenate([scaled[j] for j in range(4)], axis=1)
    scaled = jnp.concatenate(split(scaled), axis=0)

    pieces, swapped = (*pieces, last), (*swapped, last_other)
    return update(half, chip, rows, scaled, [v for pair in zip(pieces, swapped) for v in pair])


def solution(mesh):
    return jax.shard_map(
        body,
        mesh=mesh,
        in_specs=(P(("pcol", "prow"), None), P("prow", "pcol"), P()),
        out_specs=P("pcol", "prow"),
        check_vma=False,
    )
```

```python
import functools

import jax
import jax.numpy as jnp
from jax import lax
from jax.experimental import pallas as pl
from jax.experimental.pallas import tpu as pltpu
from jax.sharding import PartitionSpec as P

UP_ONE = [(c, c + 2) for c in range(6)]
DOWN_ONE = [(c, c - 2) for c in range(2, 8)]
UP_TWO = [(c, c + 2) for c in range(2, 6)]
DOWN_TWO = [(c, c - 2) for c in range(2, 6)]
TO_ENDS = [(4, 6), (5, 7), (2, 0), (3, 1)]
SIBLING = [(c, c ^ 1) for c in range(8)]
FAR = [(r, (r + 16) % 32) for r in range(32)]
PLANES = [list(range(16)), list(range(16, 32))]


def along_x(step):
    return [(r, r // 4 * 4 + (r + step) % 4) for r in range(32)]


def along_y(step):
    return [(r, r // 16 * 16 + (r + 4 * step) % 16) for r in range(32)]


def upper_part(square):
    width = square.shape[0]
    rows = lax.broadcasted_iota(jnp.int32, (width, width), 0)
    cols = lax.broadcasted_iota(jnp.int32, (width, width), 1)
    return jnp.where(cols >= rows, square, jnp.zeros_like(square))


def matmul(left, right, precision=lax.Precision.HIGHEST):
    return jnp.dot(left, right, precision=precision, preferred_element_type=jnp.float32)


def matmul_nt(left, right):
    return lax.dot_general(
        left, right, (((1,), (1,)), ((), ())),
        precision=lax.Precision.HIGH, preferred_element_type=jnp.float32,
    )


def sum_over_prow(quarters, block):
    x = lax.axis_index("prow") % 4
    count = quarters.shape[1]

    def send(value, pairs):
        return lax.ppermute(value, "prow", pairs)

    def packed(step):
        part = lax.dynamic_index_in_dim(quarters, (x + step) % 4, 0, keepdims=False)
        return jnp.concatenate([part, block], axis=0)

    total = packed(0)
    for step in (1, 2, 3):
        total = total + send(packed(step), along_x(step))
    total = total + send(total, along_y(1)) + send(total, along_y(2)) + send(total, along_y(3))
    far = send(total, FAR)
    mid = count // 2
    total = total + jnp.concatenate([far[mid:count], far[:mid], far[count:]], axis=0)
    part = total[:count]
    return jnp.stack([part, *(send(part, along_x(4 - step)) for step in (1, 2, 3))]), total[count:]


def turned(parts, start):
    return lax.dynamic_slice_in_dim(jnp.concatenate([parts, parts], axis=0), start % 4, 4, 0)


def split(value):
    high = lax.reduce_precision(value, 8, 7)
    return high.astype(jnp.bfloat16), (value - high).astype(jnp.bfloat16)


def update_kernel(where_ref, rows_ref, scaled_ref, *refs):
    out_ref = refs[-1]
    count, mid = rows_ref.shape[0], rows_ref.shape[0] // 2
    mine, above, two, below, last = (
        jnp.concatenate([refs[j][...], refs[j + 1][...]], axis=0) for j in range(0, 10, 2)
    )
    above = jnp.where(where_ref[2] == 0, last, above)
    below = jnp.where(where_ref[3] == 0, last, below)
    dot = functools.partial(jnp.dot, preferred_element_type=jnp.float32)
    change = None
    for pair, slots in enumerate(((mine, above), (two, below))):
        vectors = jnp.concatenate(slots, axis=0)
        high = vectors.astype(jnp.bfloat16)
        low = (vectors - high.astype(jnp.float32)).astype(jnp.bfloat16)
        left = scaled_ref[:, slice(256 * pair, 256 * pair + 256)]
        both = dot(left, high)
        part = both[:count] + both[count:] + dot(left[:count], low)
        change = part if change is None else change + part
    result = rows_ref[...] - change
    place = pl.multiple_of(where_ref[0] * mid, mid)
    other = pl.multiple_of((1 - where_ref[0]) * mid, mid)
    out_ref[pl.ds(place, mid), :] = result[:mid]
    out_ref[pl.ds(other, mid), :] = result[mid:]


def update(half, chip, rows, scaled, pieces, tile=1792):
    count, length = rows.shape
    where = jnp.stack(
        [half, chip, (chip != 3) * 1, (chip != 0) * 1, ((chip == 0) | (chip == 3)) * 1]
    ).astype(jnp.int32)
    streams = (None, 2, None, 3, 4)

    def piece(flag):
        if flag is None:
            return pl.BlockSpec((64, tile), lambda i, w: (0, i))
        return pl.BlockSpec((64, tile), lambda i, w: (0, i * w[flag]))

    return pl.pallas_call(
        update_kernel,
        out_shape=jax.ShapeDtypeStruct(rows.shape, jnp.float32),
        grid_spec=pltpu.PrefetchScalarGridSpec(
            num_scalar_prefetch=1,
            grid=(length // tile,),
            in_specs=[
                pl.BlockSpec((count, tile), lambda i, w: (0, i)),
                pl.BlockSpec(scaled.shape, lambda i, w: (0, 0)),
                *[piece(flag) for flag in streams for _ in range(2)],
            ],
            out_specs=pl.BlockSpec((count, tile), lambda i, w: (0, i)),
        ),
        compiler_params=pltpu.CompilerParams(vmem_limit_bytes=60 * 1024 * 1024),
        cost_estimate=pl.CostEstimate(
            flops=6 * count * 512 * length,
            bytes_accessed=length * (count * 8 + 512 * 4),
            transcendentals=0,
        ),
    )(where, rows, scaled, *pieces)


def body(eigen_rows, reflectors, tfactors):
    count = eigen_rows.shape[0]
    prow = lax.axis_index("prow")
    x, half = prow % 4, prow // 16
    column = lax.axis_index("pcol")
    chip, core = column // 2, column % 2
    length = reflectors.shape[0]
    mine = reflectors.T

    def send(value, pairs):
        return lax.ppermute(value, "pcol", pairs)

    def ordered(piece, other, axis):
        return jnp.concatenate(
            [jnp.where(core == 0, piece, other), jnp.where(core == 0, other, piece)], axis=axis
        )

    blocks = eigen_rows.reshape(count, 32, length).transpose(1, 0, 2)

    def zero_from(*values):
        return sum(jnp.minimum(jnp.abs(value[0, 0]), 0.0) for value in values).astype(jnp.int32)

    def over_plane(value):
        value = lax.all_to_all(
            value, "prow", split_axis=0, concat_axis=0, tiled=True, axis_index_groups=PLANES
        )
        return value.reshape(16 * count, length)

    below = send(mine, UP_ONE)
    above = send(mine, DOWN_ONE)
    mine_other = send(mine, SIBLING)
    leaving = lax.dynamic_slice_in_dim(blocks, (1 - half) * 16, 16, 0)
    arriving = over_plane(lax.ppermute(leaving, "prow", FAR))
    staying = over_plane(
        lax.dynamic_slice_in_dim(blocks, half * 16 + zero_from(leaving[0]), 16, 0)
    )
    below_two = send(below, UP_TWO)
    above_two = send(above, DOWN_TWO)
    last = send(jnp.where(chip == 2, below_two, above_two), TO_ENDS)
    rows = lax.dynamic_update_slice_in_dim(
        jnp.pad(staying, ((0, 16 * count), (0, 0))),
        arriving,
        16 * count + zero_from(below_two, above_two),
        0,
    )
    two = below_two + above_two

    pieces = (mine, above, two, below)
    swapped = [mine_other, *(send(piece, SIBLING) for piece in pieces[1:])]
    all_mine, all_above, all_two, all_below = (
        ordered(piece, other, 0) for piece, other in zip(pieces, swapped)
    )

    left = jnp.where(chip == 0, two, jnp.where(chip == 3, mine, above))
    right = jnp.where(chip == 0, all_above, jnp.where(chip == 1, all_below, all_two))
    cross = matmul_nt(left, right)
    on_mine, on_two = matmul_nt(rows, all_mine), matmul_nt(rows, all_two)
    on_above, on_below = matmul_nt(rows, all_above), matmul_nt(rows, all_below)
    last, cross, on_mine, on_two, on_above, on_below = lax.optimization_barrier(
        (last, cross, on_mine, on_two, on_above, on_below)
    )
    last_other = send(last, SIBLING)
    both = lax.optimization_barrier(jnp.concatenate([last, last_other], axis=0))
    on_last = matmul_nt(rows, both)
    on_last = jnp.where(core == 0, on_last, jnp.roll(on_last, 64, axis=1))
    zero = jnp.zeros_like(on_last)
    slots = jnp.stack(
        [
            on_mine,
            on_above + jnp.where(chip == 3, on_last, zero),
            on_two,
            on_below + jnp.where(chip == 0, on_last, zero),
        ]
    )
    projected, cross = sum_over_prow(slots, cross)
    cross = ordered(cross, send(cross, SIBLING), 0)
    cross = turned(
        jnp.stack(
            [cross]
            + [send(cross, [(c, (c + 2 * (4 - step)) % 8) for c in range(8)]) for step in (1, 2, 3)]
        ),
        4 - chip,
    )
    cross = jnp.concatenate(
        [
            jnp.concatenate([cross[1], cross[0]], axis=1),
            jnp.concatenate([cross[2], cross[3]], axis=1),
        ],
        axis=0,
    )
    projected = turned(projected, 8 - chip - x)
    first = jnp.concatenate([projected[0], projected[1]], axis=1)
    second = jnp.concatenate([projected[2], projected[3]], axis=1)
    scaled_second = matmul(second, upper_part(tfactors[1]).T)
    scaled_first = matmul(first - matmul(scaled_second, cross), upper_part(tfactors[0]).T)
    scaled = jnp.stack(
        [scaled_first[:, :128], scaled_first[:, 128:], scaled_second[:, :128], scaled_second[:, 128:]]
    )
    scaled = turned(scaled, chip)
    scaled = jnp.where(core == 0, scaled, jnp.roll(scaled, 64, axis=2))
    scaled = jnp.concatenate([scaled[j] for j in range(4)], axis=1)
    scaled = jnp.concatenate(split(scaled), axis=0)

    pieces, swapped = (*pieces, last), (*swapped, last_other)
    return update(half, chip, rows, scaled, [v for pair in zip(pieces, swapped) for v in pair])


def solution(mesh):
    return jax.shard_map(
        body,
        mesh=mesh,
        in_specs=(P(("pcol", "prow"), None), P("prow", "pcol"), P()),
        out_specs=P("pcol", "prow"),
        check_vma=False,
    )
```

```python
import functools

import jax
import jax.numpy as jnp
from jax import lax
from jax.experimental import pallas as pl
from jax.experimental.pallas import tpu as pltpu
from jax.sharding import PartitionSpec as P

UP_ONE = [(c, c + 2) for c in range(6)]
DOWN_ONE = [(c, c - 2) for c in range(2, 8)]
UP_TWO = [(c, c + 2) for c in range(2, 6)]
DOWN_TWO = [(c, c - 2) for c in range(2, 6)]
TO_ENDS = [(4, 6), (5, 7), (2, 0), (3, 1)]
SIBLING = [(c, c ^ 1) for c in range(8)]
FAR = [(r, (r + 16) % 32) for r in range(32)]
PLANES = [list(range(16)), list(range(16, 32))]


def along_x(step):
    return [(r, r // 4 * 4 + (r + step) % 4) for r in range(32)]


def along_y(step):
    return [(r, r // 16 * 16 + (r + 4 * step) % 16) for r in range(32)]


def upper_part(square):
    width = square.shape[0]
    rows = lax.broadcasted_iota(jnp.int32, (width, width), 0)
    cols = lax.broadcasted_iota(jnp.int32, (width, width), 1)
    return jnp.where(cols >= rows, square, jnp.zeros_like(square))


def matmul(left, right, precision=lax.Precision.HIGHEST):
    return jnp.dot(left, right, precision=precision, preferred_element_type=jnp.float32)


def matmul_nt(left, right):
    return lax.dot_general(
        left, right, (((1,), (1,)), ((), ())),
        precision=lax.Precision.HIGH, preferred_element_type=jnp.float32,
    )


def sum_over_prow(quarters, block):
    x = lax.axis_index("prow") % 4
    count = quarters.shape[1]

    def send(value, pairs):
        return lax.ppermute(value, "prow", pairs)

    def packed(step):
        part = lax.dynamic_index_in_dim(quarters, (x + step) % 4, 0, keepdims=False)
        return jnp.concatenate([part, block], axis=0)

    total = packed(0)
    for step in (1, 2, 3):
        total = total + send(packed(step), along_x(step))
    total = total + send(total, along_y(1)) + send(total, along_y(2)) + send(total, along_y(3))
    far = send(total, FAR)
    mid = count // 2
    total = total + jnp.concatenate([far[mid:count], far[:mid], far[count:]], axis=0)
    part = total[:count]
    return jnp.stack([part, *(send(part, along_x(4 - step)) for step in (1, 2, 3))]), total[count:]


def turned(parts, start):
    return lax.dynamic_slice_in_dim(jnp.concatenate([parts, parts], axis=0), start % 4, 4, 0)


def split(value):
    high = lax.reduce_precision(value, 8, 7)
    return high.astype(jnp.bfloat16), (value - high).astype(jnp.bfloat16)


def update_kernel(where_ref, rows_ref, scaled_ref, *refs):
    out_ref = refs[-1]
    count, mid = rows_ref.shape[0], rows_ref.shape[0] // 2
    mine, above, two, below, last = (
        jnp.concatenate([refs[j][...], refs[j + 1][...]], axis=0) for j in range(0, 10, 2)
    )
    above = jnp.where(where_ref[2] == 0, last, above)
    below = jnp.where(where_ref[3] == 0, last, below)
    dot = functools.partial(jnp.dot, preferred_element_type=jnp.float32)
    change = None
    for pair, slots in enumerate(((mine, above), (two, below))):
        vectors = jnp.concatenate(slots, axis=0)
        high = vectors.astype(jnp.bfloat16)
        low = (vectors - high.astype(jnp.float32)).astype(jnp.bfloat16)
        left = scaled_ref[:, slice(256 * pair, 256 * pair + 256)]
        both = dot(left, high)
        part = both[:count] + both[count:] + dot(left[:count], low)
        change = part if change is None else change + part
    result = rows_ref[...] - change
    place = pl.multiple_of(where_ref[0] * mid, mid)
    other = pl.multiple_of((1 - where_ref[0]) * mid, mid)
    out_ref[pl.ds(place, mid), :] = result[:mid]
    out_ref[pl.ds(other, mid), :] = result[mid:]


def update(half, chip, rows, scaled, pieces, tile=1792):
    count, length = rows.shape
    where = jnp.stack(
        [half, chip, (chip != 3) * 1, (chip != 0) * 1, ((chip == 0) | (chip == 3)) * 1]
    ).astype(jnp.int32)
    streams = (None, 2, None, 3, 4)

    def piece(flag):
        if flag is None:
            return pl.BlockSpec((64, tile), lambda i, w: (0, i))
        return pl.BlockSpec((64, tile), lambda i, w: (0, i * w[flag]))

    return pl.pallas_call(
        update_kernel,
        out_shape=jax.ShapeDtypeStruct(rows.shape, jnp.float32),
        grid_spec=pltpu.PrefetchScalarGridSpec(
            num_scalar_prefetch=1,
            grid=(length // tile,),
            in_specs=[
                pl.BlockSpec((count, tile), lambda i, w: (0, i)),
                pl.BlockSpec(scaled.shape, lambda i, w: (0, 0)),
                *[piece(flag) for flag in streams for _ in range(2)],
            ],
            out_specs=pl.BlockSpec((count, tile), lambda i, w: (0, i)),
        ),
        compiler_params=pltpu.CompilerParams(vmem_limit_bytes=60 * 1024 * 1024),
        cost_estimate=pl.CostEstimate(
            flops=6 * count * 512 * length,
            bytes_accessed=length * (count * 8 + 512 * 4),
            transcendentals=0,
        ),
    )(where, rows, scaled, *pieces)


def body(eigen_rows, reflectors, tfactors):
    count = eigen_rows.shape[0]
    prow = lax.axis_index("prow")
    x, half = prow % 4, prow // 16
    column = lax.axis_index("pcol")
    chip, core = column // 2, column % 2
    length = reflectors.shape[0]
    mine = reflectors.T

    def send(value, pairs):
        return lax.ppermute(value, "pcol", pairs)

    def ordered(piece, other, axis):
        return jnp.concatenate(
            [jnp.where(core == 0, piece, other), jnp.where(core == 0, other, piece)], axis=axis
        )

    blocks = eigen_rows.reshape(count, 32, length).transpose(1, 0, 2)

    def zero_from(*values):
        return sum(jnp.minimum(jnp.abs(value[0, 0]), 0.0) for value in values).astype(jnp.int32)

    def over_plane(value):
        return lax.all_to_all(
            value, "prow", split_axis=0, concat_axis=0, tiled=True, axis_index_groups=PLANES
        )

    below = send(mine, UP_ONE)
    above = send(mine, DOWN_ONE)
    mine_other = send(mine, SIBLING)
    leaving = lax.dynamic_slice_in_dim(blocks, (1 - half) * 16, 16, 0)
    arriving = over_plane(lax.ppermute(leaving, "prow", FAR))
    staying = over_plane(
        lax.dynamic_slice_in_dim(blocks, half * 16 + zero_from(leaving[0]), 16, 0)
    )
    below_two = send(below, UP_TWO)
    above_two = send(above, DOWN_TWO)
    two = jnp.where(chip >= 2, below_two, above_two)
    last = send(two, TO_ENDS)
    rows = lax.dynamic_update_slice_in_dim(
        jnp.pad(staying, ((0, 16), (0, 0), (0, 0))), arriving, 16 + zero_from(two), 0
    ).reshape(32 * count, length)

    pieces = (mine, above, two, below)
    swapped = [mine_other, *(send(piece, SIBLING) for piece in pieces[1:])]
    all_mine, all_above, all_two, all_below = (
        ordered(piece, other, 0) for piece, other in zip(pieces, swapped)
    )

    left = jnp.where(chip == 0, two, jnp.where(chip == 3, mine, above))
    right = jnp.where(chip == 0, all_above, jnp.where(chip == 1, all_below, all_two))
    cross = matmul_nt(left, right)
    on_mine, on_two = matmul_nt(rows, all_mine), matmul_nt(rows, all_two)
    on_above, on_below = matmul_nt(rows, all_above), matmul_nt(rows, all_below)
    last, cross, on_mine, on_two, on_above, on_below = lax.optimization_barrier(
        (last, cross, on_mine, on_two, on_above, on_below)
    )
    last_other = send(last, SIBLING)
    both = lax.optimization_barrier(jnp.concatenate([last, last_other], axis=0))
    on_last = matmul_nt(rows, both)
    on_last = jnp.where(core == 0, on_last, jnp.roll(on_last, 64, axis=1))
    zero = jnp.zeros_like(on_last)
    slots = jnp.stack(
        [
            on_mine,
            on_above + jnp.where(chip == 3, on_last, zero),
            on_two,
            on_below + jnp.where(chip == 0, on_last, zero),
        ]
    )
    projected, cross = sum_over_prow(slots, cross)
    cross = ordered(cross, send(cross, SIBLING), 0)
    cross = turned(
        jnp.stack(
            [cross]
            + [send(cross, [(c, (c + 2 * (4 - step)) % 8) for c in range(8)]) for step in (1, 2, 3)]
        ),
        4 - chip,
    )
    cross = jnp.concatenate(
        [
            jnp.concatenate([cross[1], cross[0]], axis=1),
            jnp.concatenate([cross[2], cross[3]], axis=1),
        ],
        axis=0,
    )
    projected = turned(projected, 8 - chip - x)
    first = jnp.concatenate([projected[0], projected[1]], axis=1)
    second = jnp.concatenate([projected[2], projected[3]], axis=1)
    scaled_second = matmul(second, upper_part(tfactors[1]).T)
    scaled_first = matmul(first - matmul(scaled_second, cross), upper_part(tfactors[0]).T)
    scaled = jnp.stack(
        [scaled_first[:, :128], scaled_first[:, 128:], scaled_second[:, :128], scaled_second[:, 128:]]
    )
    scaled = turned(scaled, chip)
    scaled = jnp.where(core == 0, scaled, jnp.roll(scaled, 64, axis=2))
    scaled = jnp.concatenate([scaled[j] for j in range(4)], axis=1)
    scaled = jnp.concatenate(split(scaled), axis=0)

    pieces, swapped = (*pieces, last), (*swapped, last_other)
    return update(half, chip, rows, scaled, [v for pair in zip(pieces, swapped) for v in pair])


def solution(mesh):
    return jax.shard_map(
        body,
        mesh=mesh,
        in_specs=(P(("pcol", "prow"), None), P("prow", "pcol"), P()),
        out_specs=P("pcol", "prow"),
        check_vma=False,
    )
```

```python
import functools

import jax
import jax.numpy as jnp
from jax import lax
from jax.experimental import pallas as pl
from jax.experimental.pallas import tpu as pltpu
from jax.sharding import PartitionSpec as P

UP_ONE = [(c, c + 2) for c in range(6)]
DOWN_ONE = [(c, c - 2) for c in range(2, 8)]
UP_TWO = [(c, c + 2) for c in range(2, 6)]
DOWN_TWO = [(c, c - 2) for c in range(2, 6)]
TO_ENDS = [(4, 6), (5, 7), (2, 0), (3, 1)]
SIBLING = [(c, c ^ 1) for c in range(8)]
FAR = [(r, (r + 16) % 32) for r in range(32)]
PLANES = [list(range(16)), list(range(16, 32))]


def along_x(step):
    return [(r, r // 4 * 4 + (r + step) % 4) for r in range(32)]


def along_y(step):
    return [(r, r // 16 * 16 + (r + 4 * step) % 16) for r in range(32)]


def upper_part(square):
    width = square.shape[0]
    rows = lax.broadcasted_iota(jnp.int32, (width, width), 0)
    cols = lax.broadcasted_iota(jnp.int32, (width, width), 1)
    return jnp.where(cols >= rows, square, jnp.zeros_like(square))


def matmul(left, right, precision=lax.Precision.HIGHEST):
    return jnp.dot(left, right, precision=precision, preferred_element_type=jnp.float32)


def matmul_nt(left, right):
    return lax.dot_general(
        left, right, (((1,), (1,)), ((), ())),
        precision=lax.Precision.HIGH, preferred_element_type=jnp.float32,
    )


def over_prow(value, pairs):
    return lax.ppermute(value, "prow", pairs)


def sum_over_plane(quarters, block=None):
    x = lax.axis_index("prow") % 4

    def packed(step):
        part = lax.dynamic_index_in_dim(quarters, (x + step) % 4, 0, keepdims=False)
        return part if block is None else jnp.concatenate([part, block], axis=0)

    total = packed(0)
    for step in (1, 2, 3):
        total = total + over_prow(packed(step), along_x(step))
    return total + sum(
        (over_prow(total, along_y(step)) for step in (2, 3)), over_prow(total, along_y(1))
    )


def in_quarters(*slots):
    return jnp.concatenate(
        [slot.reshape(2, 4, 16, 128).transpose(1, 0, 2, 3).reshape(4, 32, 128) for slot in slots],
        axis=1,
    )


def finish_sum(parts):
    x = lax.axis_index("prow") % 4
    far = over_prow(parts, FAR)
    swapped = far[:128].reshape(4, 2, 16, 128)[:, ::-1].reshape(128, 128)
    parts = parts + jnp.concatenate([swapped, far[128:]], axis=0)
    own = parts[:128]
    ring = jnp.stack([own, *(over_prow(own, along_x(4 - step)) for step in (1, 2, 3))])
    slots = turned(ring, 4 - x).reshape(4, 4, 2, 16, 128).transpose(1, 2, 0, 3, 4)
    return slots.reshape(4, 128, 128), parts[128:]


def turned(parts, start):
    return lax.dynamic_slice_in_dim(jnp.concatenate([parts, parts], axis=0), start % 4, 4, 0)


def split(value):
    high = lax.reduce_precision(value, 8, 7)
    return high.astype(jnp.bfloat16), (value - high).astype(jnp.bfloat16)


def update_kernel(where_ref, rows_ref, scaled_ref, *refs):
    out_ref = refs[-1]
    count, mid = rows_ref.shape[0], rows_ref.shape[0] // 2
    mine, above, two, below, last = (
        jnp.concatenate([refs[j][...], refs[j + 1][...]], axis=0) for j in range(0, 10, 2)
    )
    above = jnp.where(where_ref[2] == 0, last, above)
    below = jnp.where(where_ref[3] == 0, last, below)
    dot = functools.partial(jnp.dot, preferred_element_type=jnp.float32)
    change = None
    for pair, slots in enumerate(((mine, above), (two, below))):
        vectors = jnp.concatenate(slots, axis=0)
        high = vectors.astype(jnp.bfloat16)
        low = (vectors - high.astype(jnp.float32)).astype(jnp.bfloat16)
        left = scaled_ref[:, slice(256 * pair, 256 * pair + 256)]
        both = dot(left, high)
        part = both[:count] + both[count:] + dot(left[:count], low)
        change = part if change is None else change + part
    result = rows_ref[...] - change
    place = pl.multiple_of(where_ref[0] * mid, mid)
    other = pl.multiple_of((1 - where_ref[0]) * mid, mid)
    out_ref[pl.ds(place, mid), :] = result[:mid]
    out_ref[pl.ds(other, mid), :] = result[mid:]


def update(half, chip, rows, scaled, pieces, tile=1792):
    count, length = rows.shape
    where = jnp.stack(
        [half, chip, (chip != 3) * 1, (chip != 0) * 1, ((chip == 0) | (chip == 3)) * 1]
    ).astype(jnp.int32)
    streams = (None, 2, None, 3, 4)

    def piece(flag):
        if flag is None:
            return pl.BlockSpec((64, tile), lambda i, w: (0, i))
        return pl.BlockSpec((64, tile), lambda i, w: (0, i * w[flag]))

    return pl.pallas_call(
        update_kernel,
        out_shape=jax.ShapeDtypeStruct(rows.shape, jnp.float32),
        grid_spec=pltpu.PrefetchScalarGridSpec(
            num_scalar_prefetch=1,
            grid=(length // tile,),
            in_specs=[
                pl.BlockSpec((count, tile), lambda i, w: (0, i)),
                pl.BlockSpec(scaled.shape, lambda i, w: (0, 0)),
                *[piece(flag) for flag in streams for _ in range(2)],
            ],
            out_specs=pl.BlockSpec((count, tile), lambda i, w: (0, i)),
        ),
        compiler_params=pltpu.CompilerParams(vmem_limit_bytes=60 * 1024 * 1024),
        cost_estimate=pl.CostEstimate(
            flops=6 * count * 512 * length,
            bytes_accessed=length * (count * 8 + 512 * 4),
            transcendentals=0,
        ),
    )(where, rows, scaled, *pieces)


def body(eigen_rows, reflectors, tfactors):
    count = eigen_rows.shape[0]
    prow = lax.axis_index("prow")
    x, half = prow % 4, prow // 16
    column = lax.axis_index("pcol")
    chip, core = column // 2, column % 2
    length = reflectors.shape[0]
    mine = reflectors.T

    def send(value, pairs):
        return lax.ppermute(value, "pcol", pairs)

    def ordered(piece, other, axis):
        return jnp.concatenate(
            [jnp.where(core == 0, piece, other), jnp.where(core == 0, other, piece)], axis=axis
        )

    blocks = eigen_rows.reshape(count, 32, length).transpose(1, 0, 2)

    def zero_from(*values):
        return sum(jnp.minimum(jnp.abs(value[0, 0]), 0.0) for value in values).astype(jnp.int32)

    def over_plane(value):
        return lax.all_to_all(
            value, "prow", split_axis=0, concat_axis=0, tiled=True, axis_index_groups=PLANES
        )

    below = send(mine, UP_ONE)
    above = send(mine, DOWN_ONE)
    mine_other = send(mine, SIBLING)
    leaving = lax.dynamic_slice_in_dim(blocks, (1 - half) * 16, 16, 0)
    arriving = over_plane(lax.ppermute(leaving, "prow", FAR))
    staying = over_plane(
        lax.dynamic_slice_in_dim(blocks, half * 16 + zero_from(leaving[0]), 16, 0)
    )
    below_two = send(below, UP_TWO)
    above_two = send(above, DOWN_TWO)
    two = jnp.where(chip >= 2, below_two, above_two)
    last = send(two, TO_ENDS)
    rows = lax.dynamic_update_slice_in_dim(
        jnp.pad(staying, ((0, 16), (0, 0), (0, 0))), arriving, 16 + zero_from(two), 0
    ).reshape(32 * count, length)

    pieces = (mine, above, two, below)
    swapped = [mine_other, *(send(piece, SIBLING) for piece in pieces[1:])]
    all_mine, all_above, all_two, all_below = (
        ordered(piece, other, 0) for piece, other in zip(pieces, swapped)
    )

    left = jnp.where(chip == 0, two, jnp.where(chip == 3, mine, above))
    right = jnp.where(chip == 0, all_above, jnp.where(chip == 1, all_below, all_two))
    cross = matmul_nt(left, right)
    on_mine, on_two = matmul_nt(rows, all_mine), matmul_nt(rows, all_two)
    on_above, on_below = matmul_nt(rows, all_above), matmul_nt(rows, all_below)
    on_mine, on_two, on_above, on_below = lax.optimization_barrier(
        (on_mine, on_two, on_above, on_below)
    )
    early = sum_over_plane(in_quarters(on_mine, on_two), cross)
    last = lax.dynamic_update_slice(last, last[:8, :128], (zero_from(early), 0))
    last_other = send(last, SIBLING)
    both = lax.optimization_barrier(jnp.concatenate([last, last_other], axis=0))
    on_last = lax.optimization_barrier(matmul_nt(rows, both))
    on_last = jnp.where(core == 0, on_last, jnp.roll(on_last, 64, axis=1))
    zero = jnp.zeros_like(on_last)
    late = sum_over_plane(
        in_quarters(
            on_above + jnp.where(chip == 3, on_last, zero),
            on_below + jnp.where(chip == 0, on_last, zero),
        )
    )
    (above_sum, below_sum, mine_sum, two_sum), cross = finish_sum(
        jnp.concatenate([late, early], axis=0)
    )
    projected = jnp.stack([mine_sum, above_sum, two_sum, below_sum])
    cross = ordered(cross, send(cross, SIBLING), 0)
    cross = turned(
        jnp.stack(
            [cross]
            + [send(cross, [(c, (c + 2 * (4 - step)) % 8) for c in range(8)]) for step in (1, 2, 3)]
        ),
        4 - chip,
    )
    cross = jnp.concatenate(
        [
            jnp.concatenate([cross[1], cross[0]], axis=1),
            jnp.concatenate([cross[2], cross[3]], axis=1),
        ],
        axis=0,
    )
    projected = turned(projected, 4 - chip)
    first = jnp.concatenate([projected[0], projected[1]], axis=1)
    second = jnp.concatenate([projected[2], projected[3]], axis=1)
    scaled_second = matmul(second, upper_part(tfactors[1]).T)
    scaled_first = matmul(first - matmul(scaled_second, cross), upper_part(tfactors[0]).T)
    scaled = jnp.stack(
        [scaled_first[:, :128], scaled_first[:, 128:], scaled_second[:, :128], scaled_second[:, 128:]]
    )
    scaled = turned(scaled, chip)
    scaled = jnp.where(core == 0, scaled, jnp.roll(scaled, 64, axis=2))
    scaled = jnp.concatenate([scaled[j] for j in range(4)], axis=1)
    scaled = jnp.concatenate(split(scaled), axis=0)

    pieces, swapped = (*pieces, last), (*swapped, last_other)
    return update(half, chip, rows, scaled, [v for pair in zip(pieces, swapped) for v in pair])


def solution(mesh):
    return jax.shard_map(
        body,
        mesh=mesh,
        in_specs=(P(("pcol", "prow"), None), P("prow", "pcol"), P()),
        out_specs=P("pcol", "prow"),
        check_vma=False,
    )
```

```python
import functools

import jax
import jax.numpy as jnp
from jax import lax
from jax.experimental import pallas as pl
from jax.experimental.pallas import tpu as pltpu
from jax.sharding import PartitionSpec as P

UP_ONE = [(c, c + 2) for c in range(6)]
DOWN_ONE = [(c, c - 2) for c in range(2, 8)]
UP_TWO = [(c, c + 2) for c in range(2, 6)]
DOWN_TWO = [(c, c - 2) for c in range(2, 6)]
TO_ENDS = [(4, 6), (5, 7), (2, 0), (3, 1)]
SIBLING = [(c, c ^ 1) for c in range(8)]
FAR = [(r, (r + 16) % 32) for r in range(32)]
PLANES = [list(range(16)), list(range(16, 32))]


def along_x(step):
    return [(r, r // 4 * 4 + (r + step) % 4) for r in range(32)]


def along_y(step):
    return [(r, r // 16 * 16 + (r + 4 * step) % 16) for r in range(32)]


def upper_part(square):
    width = square.shape[0]
    rows = lax.broadcasted_iota(jnp.int32, (width, width), 0)
    cols = lax.broadcasted_iota(jnp.int32, (width, width), 1)
    return jnp.where(cols >= rows, square, jnp.zeros_like(square))


def matmul(left, right, precision=lax.Precision.HIGHEST):
    return jnp.dot(left, right, precision=precision, preferred_element_type=jnp.float32)


def matmul_nt(left, right):
    return lax.dot_general(
        left, right, (((1,), (1,)), ((), ())),
        precision=lax.Precision.HIGH, preferred_element_type=jnp.float32,
    )


def sum_over_prow(quarters, block):
    x = lax.axis_index("prow") % 4
    count = quarters.shape[1]

    def send(value, pairs):
        return lax.ppermute(value, "prow", pairs)

    def packed(step):
        part = lax.dynamic_index_in_dim(quarters, (x + step) % 4, 0, keepdims=False)
        return jnp.concatenate([part, block], axis=0)

    total = packed(0)
    for step in (1, 2, 3):
        total = total + send(packed(step), along_x(step))
    total = total + send(total, along_y(1)) + send(total, along_y(2)) + send(total, along_y(3))
    far = send(total, FAR)
    mid = count // 2
    total = total + jnp.concatenate([far[mid:count], far[:mid], far[count:]], axis=0)
    part = total[:count]
    return jnp.stack([part, *(send(part, along_x(4 - step)) for step in (1, 2, 3))]), total[count:]


def turned(parts, start):
    return lax.dynamic_slice_in_dim(jnp.concatenate([parts, parts], axis=0), start % 4, 4, 0)


def split(value):
    high = lax.reduce_precision(value, 8, 7)
    return high.astype(jnp.bfloat16), (value - high).astype(jnp.bfloat16)


def update_kernel(where_ref, rows_ref, scaled_ref, *refs):
    out_ref = refs[-1]
    count, mid = rows_ref.shape[0], rows_ref.shape[0] // 2
    mine, above, two, below, last = (
        jnp.concatenate([refs[j][...], refs[j + 1][...]], axis=0) for j in range(0, 10, 2)
    )
    above = jnp.where(where_ref[2] == 0, last, above)
    below = jnp.where(where_ref[3] == 0, last, below)
    dot = functools.partial(jnp.dot, preferred_element_type=jnp.float32)
    change = None
    for pair, slots in enumerate(((mine, above), (two, below))):
        vectors = jnp.concatenate(slots, axis=0)
        high = vectors.astype(jnp.bfloat16)
        low = (vectors - high.astype(jnp.float32)).astype(jnp.bfloat16)
        left = scaled_ref[:, slice(256 * pair, 256 * pair + 256)]
        both = dot(left, high)
        part = both[:count] + both[count:] + dot(left[:count], low)
        change = part if change is None else change + part
    result = rows_ref[...] - change
    place = pl.multiple_of(where_ref[0] * mid, mid)
    other = pl.multiple_of((1 - where_ref[0]) * mid, mid)
    out_ref[pl.ds(place, mid), :] = result[:mid]
    out_ref[pl.ds(other, mid), :] = result[mid:]


def update(half, chip, rows, scaled, pieces, tile=1792):
    count, length = rows.shape
    where = jnp.stack(
        [half, chip, (chip != 3) * 1, (chip != 0) * 1, ((chip == 0) | (chip == 3)) * 1]
    ).astype(jnp.int32)
    streams = (None, 2, None, 3, 4)

    def piece(flag):
        if flag is None:
            return pl.BlockSpec((64, tile), lambda i, w: (0, i))
        return pl.BlockSpec((64, tile), lambda i, w: (0, i * w[flag]))

    return pl.pallas_call(
        update_kernel,
        out_shape=jax.ShapeDtypeStruct(rows.shape, jnp.float32),
        grid_spec=pltpu.PrefetchScalarGridSpec(
            num_scalar_prefetch=1,
            grid=(length // tile,),
            in_specs=[
                pl.BlockSpec((count, tile), lambda i, w: (0, i)),
                pl.BlockSpec(scaled.shape, lambda i, w: (0, 0)),
                *[piece(flag) for flag in streams for _ in range(2)],
            ],
            out_specs=pl.BlockSpec((count, tile), lambda i, w: (0, i)),
        ),
        compiler_params=pltpu.CompilerParams(vmem_limit_bytes=60 * 1024 * 1024),
        cost_estimate=pl.CostEstimate(
            flops=6 * count * 512 * length,
            bytes_accessed=length * (count * 8 + 512 * 4),
            transcendentals=0,
        ),
    )(where, rows, scaled, *pieces)


def body(eigen_rows, reflectors, tfactors):
    count = eigen_rows.shape[0]
    prow = lax.axis_index("prow")
    x, half = prow % 4, prow // 16
    column = lax.axis_index("pcol")
    chip, core = column // 2, column % 2
    length = reflectors.shape[0]
    mine = reflectors.T

    def send(value, pairs):
        return lax.ppermute(value, "pcol", pairs)

    def ordered(piece, other, axis):
        return jnp.concatenate(
            [jnp.where(core == 0, piece, other), jnp.where(core == 0, other, piece)], axis=axis
        )

    blocks = eigen_rows.reshape(count, 32, length).transpose(1, 0, 2)

    def zero_from(*values):
        return sum(jnp.minimum(jnp.abs(value[0, 0]), 0.0) for value in values).astype(jnp.int32)

    def over_plane(value):
        return lax.all_to_all(
            value, "prow", split_axis=0, concat_axis=0, tiled=True, axis_index_groups=PLANES
        )

    below = send(mine, UP_ONE)
    above = send(mine, DOWN_ONE)
    mine_other = send(mine, SIBLING)
    leaving = lax.dynamic_slice_in_dim(blocks, (1 - half) * 16, 16, 0)
    arriving = over_plane(lax.ppermute(leaving, "prow", FAR))
    staying = over_plane(
        lax.dynamic_slice_in_dim(blocks, half * 16 + zero_from(leaving[0]), 16, 0)
    )
    below_two = send(below, UP_TWO)
    above_two = send(above, DOWN_TWO)
    two = jnp.where(chip >= 2, below_two, above_two)
    last = send(two, TO_ENDS)
    rows = lax.dynamic_update_slice_in_dim(
        jnp.pad(staying, ((0, 16), (0, 0), (0, 0))), arriving, 16 + zero_from(two), 0
    ).reshape(32 * count, length)

    pieces = (mine, above, two, below)
    swapped = [mine_other, *(send(piece, SIBLING) for piece in pieces[1:])]
    all_mine, all_above, all_two, all_below = (
        ordered(piece, other, 0) for piece, other in zip(pieces, swapped)
    )

    left = jnp.where(chip == 0, two, jnp.where(chip == 3, mine, above))
    right = jnp.where(chip == 0, all_above, jnp.where(chip == 1, all_below, all_two))
    cross = matmul_nt(left, right)
    cross = ordered(cross, send(cross, SIBLING), 0)
    on_mine, on_two = matmul_nt(rows, all_mine), matmul_nt(rows, all_two)
    on_above, on_below = matmul_nt(rows, all_above), matmul_nt(rows, all_below)
    last, cross, on_mine, on_two, on_above, on_below = lax.optimization_barrier(
        (last, cross, on_mine, on_two, on_above, on_below)
    )
    last_other = send(last, SIBLING)
    both = lax.optimization_barrier(jnp.concatenate([last, last_other], axis=0))
    on_last = matmul_nt(rows, both)
    on_last = jnp.where(core == 0, on_last, jnp.roll(on_last, 64, axis=1))
    zero = jnp.zeros_like(on_last)
    slots = jnp.stack(
        [
            on_mine,
            on_above + jnp.where(chip == 3, on_last, zero),
            on_two,
            on_below + jnp.where(chip == 0, on_last, zero),
        ]
    )
    projected, cross = sum_over_prow(slots, cross)
    cross = turned(
        jnp.stack(
            [cross]
            + [send(cross, [(c, (c + 2 * (4 - step)) % 8) for c in range(8)]) for step in (1, 2, 3)]
        ),
        4 - chip,
    )
    cross = jnp.concatenate(
        [
            jnp.concatenate([cross[1], cross[0]], axis=1),
            jnp.concatenate([cross[2], cross[3]], axis=1),
        ],
        axis=0,
    )
    projected = turned(projected, 8 - chip - x)
    first = jnp.concatenate([projected[0], projected[1]], axis=1)
    second = jnp.concatenate([projected[2], projected[3]], axis=1)
    scaled_second = matmul(second, upper_part(tfactors[1]).T)
    scaled_first = matmul(first - matmul(scaled_second, cross), upper_part(tfactors[0]).T)
    scaled = jnp.stack(
        [scaled_first[:, :128], scaled_first[:, 128:], scaled_second[:, :128], scaled_second[:, 128:]]
    )
    scaled = turned(scaled, chip)
    scaled = jnp.where(core == 0, scaled, jnp.roll(scaled, 64, axis=2))
    scaled = jnp.concatenate([scaled[j] for j in range(4)], axis=1)
    scaled = jnp.concatenate(split(scaled), axis=0)

    pieces, swapped = (*pieces, last), (*swapped, last_other)
    return update(half, chip, rows, scaled, [v for pair in zip(pieces, swapped) for v in pair])


def solution(mesh):
    return jax.shard_map(
        body,
        mesh=mesh,
        in_specs=(P(("pcol", "prow"), None), P("prow", "pcol"), P()),
        out_specs=P("pcol", "prow"),
        check_vma=False,
    )
```

```python
import functools

import jax
import jax.numpy as jnp
from jax import lax
from jax.experimental import pallas as pl
from jax.experimental.pallas import tpu as pltpu
from jax.sharding import PartitionSpec as P

UP_ONE = [(c, c + 2) for c in range(6)]
DOWN_ONE = [(c, c - 2) for c in range(2, 8)]
UP_TWO = [(c, c + 2) for c in range(2, 6)]
DOWN_TWO = [(c, c - 2) for c in range(2, 6)]
TO_ENDS = [(4, 6), (5, 7), (2, 0), (3, 1)]
SIBLING = [(c, c ^ 1) for c in range(8)]
FAR = [(r, (r + 16) % 32) for r in range(32)]
PLANES = [list(range(16)), list(range(16, 32))]


def along_x(step):
    return [(r, r // 4 * 4 + (r + step) % 4) for r in range(32)]


def along_y(step):
    return [(r, r // 16 * 16 + (r + 4 * step) % 16) for r in range(32)]


def upper_part(square):
    width = square.shape[0]
    rows = lax.broadcasted_iota(jnp.int32, (width, width), 0)
    cols = lax.broadcasted_iota(jnp.int32, (width, width), 1)
    return jnp.where(cols >= rows, square, jnp.zeros_like(square))


def matmul(left, right, precision=lax.Precision.HIGHEST):
    return jnp.dot(left, right, precision=precision, preferred_element_type=jnp.float32)


def matmul_nt(left, right):
    return lax.dot_general(
        left, right, (((1,), (1,)), ((), ())),
        precision=lax.Precision.HIGH, preferred_element_type=jnp.float32,
    )


def sum_over_prow(quarters, block):
    x = lax.axis_index("prow") % 4
    count = quarters.shape[1]

    def send(value, pairs):
        return lax.ppermute(value, "prow", pairs)

    def packed(step):
        part = lax.dynamic_index_in_dim(quarters, (x + step) % 4, 0, keepdims=False)
        return jnp.concatenate([part, block], axis=0)

    total = packed(0)
    for step in (1, 2, 3):
        total = total + send(packed(step), along_x(step))
    total = total + send(total, along_y(1)) + send(total, along_y(2)) + send(total, along_y(3))
    far = send(total, FAR)
    mid = count // 2
    total = total + jnp.concatenate([far[mid:count], far[:mid], far[count:]], axis=0)
    part = total[:count]
    return jnp.stack([part, *(send(part, along_x(4 - step)) for step in (1, 2, 3))]), total[count:]


def turned(parts, start):
    return lax.dynamic_slice_in_dim(jnp.concatenate([parts, parts], axis=0), start % 4, 4, 0)


def split(value):
    high = lax.reduce_precision(value, 8, 7)
    return high.astype(jnp.bfloat16), (value - high).astype(jnp.bfloat16)


def update_kernel(where_ref, rows_ref, scaled_ref, *refs):
    out_ref = refs[-1]
    count, mid = rows_ref.shape[0], rows_ref.shape[0] // 2
    mine, above, two, below, last = (
        jnp.concatenate([refs[j][...], refs[j + 1][...]], axis=0) for j in range(0, 10, 2)
    )
    above = jnp.where(where_ref[2] == 0, last, above)
    below = jnp.where(where_ref[3] == 0, last, below)
    dot = functools.partial(jnp.dot, preferred_element_type=jnp.float32)
    change = None
    for pair, slots in enumerate(((mine, above), (two, below))):
        vectors = jnp.concatenate(slots, axis=0)
        high = vectors.astype(jnp.bfloat16)
        low = (vectors - high.astype(jnp.float32)).astype(jnp.bfloat16)
        left = scaled_ref[:, slice(256 * pair, 256 * pair + 256)]
        both = dot(left, high)
        part = both[:count] + both[count:] + dot(left[:count], low)
        change = part if change is None else change + part
    result = rows_ref[...] - change
    place = pl.multiple_of(where_ref[0] * mid, mid)
    other = pl.multiple_of((1 - where_ref[0]) * mid, mid)
    out_ref[pl.ds(place, mid), :] = result[:mid]
    out_ref[pl.ds(other, mid), :] = result[mid:]


def update(half, chip, rows, scaled, pieces, tile=1792):
    count, length = rows.shape
    where = jnp.stack(
        [half, chip, (chip != 3) * 1, (chip != 0) * 1, ((chip == 0) | (chip == 3)) * 1]
    ).astype(jnp.int32)
    streams = (None, 2, None, 3, 4)

    def piece(flag):
        if flag is None:
            return pl.BlockSpec((64, tile), lambda i, w: (0, i))
        return pl.BlockSpec((64, tile), lambda i, w: (0, i * w[flag]))

    return pl.pallas_call(
        update_kernel,
        out_shape=jax.ShapeDtypeStruct(rows.shape, jnp.float32),
        grid_spec=pltpu.PrefetchScalarGridSpec(
            num_scalar_prefetch=1,
            grid=(length // tile,),
            in_specs=[
                pl.BlockSpec((count, tile), lambda i, w: (0, i)),
                pl.BlockSpec(scaled.shape, lambda i, w: (0, 0)),
                *[piece(flag) for flag in streams for _ in range(2)],
            ],
            out_specs=pl.BlockSpec((count, tile), lambda i, w: (0, i)),
        ),
        compiler_params=pltpu.CompilerParams(vmem_limit_bytes=60 * 1024 * 1024),
        cost_estimate=pl.CostEstimate(
            flops=6 * count * 512 * length,
            bytes_accessed=length * (count * 8 + 512 * 4),
            transcendentals=0,
        ),
    )(where, rows, scaled, *pieces)


def body(eigen_rows, reflectors, tfactors):
    count = eigen_rows.shape[0]
    prow = lax.axis_index("prow")
    x, half = prow % 4, prow // 16
    column = lax.axis_index("pcol")
    chip, core = column // 2, column % 2
    length = reflectors.shape[0]
    mine = reflectors.T

    def send(value, pairs):
        return lax.ppermute(value, "pcol", pairs)

    def ordered(piece, other, axis):
        return jnp.concatenate(
            [jnp.where(core == 0, piece, other), jnp.where(core == 0, other, piece)], axis=axis
        )

    blocks = eigen_rows.reshape(count, 32, length).transpose(1, 0, 2)

    def zero_from(*values):
        return sum(jnp.minimum(jnp.abs(value[0, 0]), 0.0) for value in values).astype(jnp.int32)

    def over_plane(value):
        return lax.all_to_all(
            value, "prow", split_axis=0, concat_axis=0, tiled=True, axis_index_groups=PLANES
        )

    below = send(mine, UP_ONE)
    above = send(mine, DOWN_ONE)
    mine_other = send(mine, SIBLING)
    leaving = lax.dynamic_slice_in_dim(blocks, (1 - half) * 16, 16, 0)
    arriving = over_plane(lax.ppermute(leaving, "prow", FAR))
    staying = over_plane(
        lax.dynamic_slice_in_dim(blocks, half * 16 + zero_from(leaving[0]), 16, 0)
    )
    below_two = send(below, UP_TWO)
    above_two = send(above, DOWN_TWO)
    two = jnp.where(chip >= 2, below_two, above_two)
    last = send(two, TO_ENDS)
    rows = lax.dynamic_update_slice_in_dim(
        jnp.pad(staying, ((0, 16), (0, 0), (0, 0))), arriving, 16 + zero_from(two), 0
    ).reshape(32 * count, length)

    pieces = (mine, above, two, below)
    swapped = [mine_other, *(send(piece, SIBLING) for piece in pieces[1:])]
    all_mine, all_above, all_two, all_below = (
        ordered(piece, other, 0) for piece, other in zip(pieces, swapped)
    )

    left = jnp.where(chip == 0, two, jnp.where(chip == 3, mine, above))
    right = jnp.where(chip == 0, all_above, jnp.where(chip == 1, all_below, all_two))
    cross = matmul_nt(left, right)
    on_mine, on_two = matmul_nt(rows, all_mine), matmul_nt(rows, all_two)
    on_above, on_below = matmul_nt(rows, all_above), matmul_nt(rows, all_below)
    last, cross, on_mine, on_two, on_above, on_below = lax.optimization_barrier(
        (last, cross, on_mine, on_two, on_above, on_below)
    )
    last_other = send(last, SIBLING)
    both = lax.optimization_barrier(ordered(last, last_other, 0))
    on_last = matmul_nt(rows, both)
    zero = jnp.zeros_like(on_last)
    slots = jnp.stack(
        [
            on_mine,
            on_above + jnp.where(chip == 3, on_last, zero),
            on_two,
            on_below + jnp.where(chip == 0, on_last, zero),
        ]
    )
    projected, cross = sum_over_prow(slots, cross)
    cross = ordered(cross, send(cross, SIBLING), 0)
    cross = turned(
        jnp.stack(
            [cross]
            + [send(cross, [(c, (c + 2 * (4 - step)) % 8) for c in range(8)]) for step in (1, 2, 3)]
        ),
        4 - chip,
    )
    cross = jnp.concatenate(
        [
            jnp.concatenate([cross[1], cross[0]], axis=1),
            jnp.concatenate([cross[2], cross[3]], axis=1),
        ],
        axis=0,
    )
    projected = turned(projected, 8 - chip - x)
    first = jnp.concatenate([projected[0], projected[1]], axis=1)
    second = jnp.concatenate([projected[2], projected[3]], axis=1)
    scaled_second = matmul(second, upper_part(tfactors[1]).T)
    scaled_first = matmul(first - matmul(scaled_second, cross), upper_part(tfactors[0]).T)
    scaled = jnp.stack(
        [scaled_first[:, :128], scaled_first[:, 128:], scaled_second[:, :128], scaled_second[:, 128:]]
    )
    scaled = turned(scaled, chip)
    scaled = jnp.where(core == 0, scaled, jnp.roll(scaled, 64, axis=2))
    scaled = jnp.concatenate([scaled[j] for j in range(4)], axis=1)
    scaled = jnp.concatenate(split(scaled), axis=0)

    pieces, swapped = (*pieces, last), (*swapped, last_other)
    return update(half, chip, rows, scaled, [v for pair in zip(pieces, swapped) for v in pair])


def solution(mesh):
    return jax.shard_map(
        body,
        mesh=mesh,
        in_specs=(P(("pcol", "prow"), None), P("prow", "pcol"), P()),
        out_specs=P("pcol", "prow"),
        check_vma=False,
    )
```
